512 devices in a mesh: xi: 16 (over z), eta: 8 (over y, core), zeta: 4 (over x).
Axes of the slice: x: 4, y: 4, z: 16, core: 2. Of those that a mesh axis runs over, the one named last changes fastest.
Arguments:
- residual: float32 [5, 32, 128, 1024], P(None, 'zeta', 'xi', 'eta'), may hold values from -6 to 6
- flow_state: float32 [5, 32, 128, 1024], P(None, 'zeta', 'xi', 'eta'), may hold values from -6 to 6
- factors_zeta: float32 [3, 5, 32, 128, 1024], P(None, None, 'zeta', 'xi', 'eta'), may hold values from -1.5 to 1.5, as said below
- factors_eta: float32 [3, 5, 32, 128, 1024], P(None, None, 'zeta', 'xi', 'eta'), may hold values from -1.5 to 1.5, as said below
- factors_xi: float32 [3, 5, 32, 128, 1024], P(None, None, 'zeta', 'xi', 'eta'), may hold values from -1.5 to 1.5, as said below
Outputs:
- update: float32 [5, 32, 128, 1024], P(None, 'zeta', 'xi', 'eta')
The draws below stay inside these ranges and needn't reach their ends.
Inputs may be any that keep to these rules, and one draw needn't show every extreme that they name: `factors_zeta`: F[g,2] is positive; the operator of each line is nonsingular. `factors_eta`: F[g,2] is positive; the operator of each line is nonsingular. `factors_xi`: F[g,2] is positive; the operator of each line is nonsingular.
All inputs are finite; a program needn't handle non-finite values.
Results may differ from the reference program's by a relative error of at most 0.000053.
Values sent between devices are 32-bit elements; how exact they have to be, the bound alone decides.
No kernel may reach another device: no remote copies, remote signals or barrier semaphores. Data moves between devices by JAX's collectives and lax.ppermute only.
A program may use at most 128 MiB of HBM per device.

```python
import jax
import jax.numpy as jnp
from jax import lax

CZ = 8
CX = 8
CY = 128
NZ = 32
NX = 128
NY = 1024


def line_speeds(complete_extent, line_dimension, block_extent, slow_flag, initial_random_key, middle_random_key, final_random_key, pulse_random_key, magnitude_key):
    line_length = complete_extent[line_dimension]
    position = lax.broadcasted_iota(jnp.int32, complete_extent, line_dimension)
    group_row = lax.broadcasted_iota(jnp.int32, complete_extent, 0)
    blocks = line_length // block_extent
    rough = jax.random.uniform(initial_random_key, complete_extent, jnp.float32, 0.6, 1.4)
    device_table = jnp.exp(jax.random.uniform(middle_random_key, (3 * blocks,), jnp.float32, -0.7, 0.7))
    device_factor = jnp.take(device_table, group_row * blocks + position // block_extent)
    fast_rate = jax.random.uniform(final_random_key, (3,), jnp.float32, 1.0 / 50.0, 1.0 / 30.0)
    slow_rate = 1.5 / line_length
    base_rate = jnp.where(slow_flag, slow_rate, fast_rate)
    falloff_speed = base_rate[:, None, None, None] * rough * device_factor
    pulse_event = jax.random.randint(pulse_random_key, complete_extent, 0, line_length) < 2
    reduction_multiplier = jax.random.uniform(magnitude_key, complete_extent, jnp.float32, 0.5, 0.8)
    keep_fraction = jnp.exp(-falloff_speed) * jnp.where(pulse_event, reduction_multiplier, 1.0)
    return (falloff_speed, keep_fraction)


def line_factors(key, line_dimension, block_extent):
    complete_extent = (3, NZ, NX, NY)
    line_length = complete_extent[line_dimension]
    subkeys = jax.random.split(key, 14)
    position = lax.broadcasted_iota(jnp.int32, complete_extent, line_dimension)
    fast_group = jax.random.randint(subkeys[0], (), 0, 3)
    slow_flag = jnp.arange(3) != fast_group
    rate_low, retain_low = line_speeds(complete_extent, line_dimension, block_extent, slow_flag, subkeys[1], subkeys[2], subkeys[3], subkeys[4], subkeys[5])
    rate_high, retain_high = line_speeds(complete_extent, line_dimension, block_extent, slow_flag, subkeys[6], subkeys[7], subkeys[8], subkeys[9], subkeys[10])
    mix_low = jax.random.uniform(subkeys[11], complete_extent, jnp.float32, -0.5, 0.5)
    mix_high = jax.random.uniform(subkeys[12], complete_extent, jnp.float32, -0.5, 0.5)
    before = jnp.roll(retain_low, 1, line_dimension) * (position > 0).astype(jnp.float32)
    after = jnp.roll(retain_high, -1, line_dimension) * (position < line_length - 1).astype(jnp.float32)
    pivot = jax.random.uniform(subkeys[13], complete_extent, jnp.float32, 0.5, 1.5) * 2.0 * jnp.sqrt(rate_low * rate_high)
    pivot = jnp.minimum(pivot, 1.45)
    return jnp.stack([-(retain_low + mix_low), mix_low * before, pivot, -(retain_high + mix_high), mix_high * after], 1)


def draw_factors_zeta(key, part):
    return line_factors(jax.random.fold_in(key, 11), 1, CZ)


def draw_factors_eta(key, part):
    return line_factors(jax.random.fold_in(key, 13), 3, CY)


def draw_factors_xi(key, part):
    return line_factors(jax.random.fold_in(key, 17), 2, CX)


def level_of(own_key, extent, cuts, smallest, largest):
    level, own = 1.0, jax.random.fold_in(own_key, 6)
    for dim, shards_of in cuts:
        heights = jnp.exp(jax.random.uniform(jax.random.fold_in(own, dim), (shards_of,), jnp.float32, smallest / len(cuts), largest / len(cuts)))
        level = level * jnp.repeat(heights, extent[dim] // shards_of).reshape([-1 if axis == dim else 1 for axis in range(len(extent))])
    return level


def noise(rng, shape, scale, most, cuts=(), kind=jnp.bfloat16):
    result = scale * jax.random.normal(rng, shape, jnp.float32)
    if cuts:
        result = result * level_of(rng, shape, cuts, -0.22, 0.18)
    return jnp.clip(result, -most, most).astype(kind)


def setup_inputs(seed: int = 0) -> dict:
    keys = jax.random.split(jax.random.key(seed), 6)
    return {
        "residual": noise(keys[0], (5, NZ, NX, NY), 1.0, 6.0, ((1, 4), (2, 16), (3, 8)), jnp.float32),
        "flow_state": noise(keys[1], (5, NZ, NX, NY), 1.0, 6.0, ((1, 4), (2, 16), (3, 8)), jnp.float32),
        "factors_zeta": draw_factors_zeta(jax.random.fold_in(keys[5], 71), 0),
        "factors_eta": draw_factors_eta(jax.random.fold_in(keys[5], 71), 0),
        "factors_xi": draw_factors_xi(jax.random.fold_in(keys[5], 71), 0),
    }


field_group = (0, 0, 0, 1, 2)
stencil_weights = (1.0, -4.0, 6.0, -4.0, 1.0)
dissipation = 0.05


def run_sweep(values, lead_row, first_row, second_row, line_axis, backward):
    columns = [jnp.moveaxis(array_item, line_axis, 0) for array_item in (values, lead_row, first_row, second_row)]
    if backward:
        columns = [jnp.flip(array_item, 0) for array_item in columns]
    zero_state = jnp.zeros_like(columns[0][0])

    def advance(carried, current):
        recent, before_last = carried
        value, scale, coef_one, coef_two = current
        updated = scale * value - coef_one * recent - coef_two * before_last
        return (updated, recent), updated

    final_state, solved = lax.scan(advance, (zero_state, zero_state), tuple(columns))
    if backward:
        solved = jnp.flip(solved, 0)
    return jnp.moveaxis(solved, 0, line_axis)


def reference(residual, flow_state, factors_zeta, factors_eta, factors_xi):
    padded = jnp.pad(flow_state, ((0, 0), (2, 2), (2, 2), (2, 2)))
    zeta_cells, xi_cells, eta_cells = flow_state.shape[1:]
    dissipated = jnp.zeros_like(flow_state)
    for position, weight in enumerate(stencil_weights):
        dissipated = dissipated + weight * (
            padded[:, position:position + zeta_cells, 2:2 + xi_cells, 2:2 + eta_cells]
            + padded[:, 2:2 + zeta_cells, position:position + xi_cells, 2:2 + eta_cells]
            + padded[:, 2:2 + zeta_cells, 2:2 + xi_cells, position:position + eta_cells])
    source = residual - dissipation * dissipated
    results = []
    for field in range(5):
        group_index = field_group[field]
        value = source[field]
        for factors, line_axis in ((factors_zeta, 0), (factors_eta, 2), (factors_xi, 1)):
            factor_group = factors[group_index]
            value = run_sweep(value, jnp.ones_like(value), factor_group[0], factor_group[1], line_axis, False)
            value = run_sweep(value, factor_group[2], factor_group[3], factor_group[4], line_axis, True)
        results.append(value)
    return jnp.stack(results, 0)
```

```python
import jax
import jax.numpy as jnp
from jax import lax
from jax.experimental import pallas as pl
from jax.experimental.pallas import tpu as pltpu
from jax.sharding import PartitionSpec as P

dissipation = 0.05
ZETA, ETA, XI = 4, 8, 16
LANES = 128
field_slot = ((0, 0), (1, 0), (2, 0), (0, 1), (1, 1))
field_group = (0, 0, 0, 1, 2)
CHUNKS = 8
STEPS = LANES // CHUNKS


def f32(*shape):
    return jax.ShapeDtypeStruct(shape, jnp.float32)


def vmem(*shape):
    return pltpu.VMEM(shape, jnp.float32)


def call(body, outs, *args, scratch=(), name=None, cost=20000, aliases={}):
    return pl.pallas_call(
        body,
        out_shape=outs,
        in_specs=[pl.BlockSpec(memory_space=pltpu.VMEM)] * len(args),
        out_specs=jax.tree.map(lambda _: pl.BlockSpec(memory_space=pltpu.VMEM), outs),
        scratch_shapes=list(scratch),
        input_output_aliases=aliases,
        name=name,
        cost_estimate=pl.CostEstimate(flops=cost * 1000, bytes_accessed=cost * 100, transcendentals=0),
        compiler_params=pltpu.CompilerParams(vmem_limit_bytes=16 << 20),
    )(*(pltpu.with_memory_space_constraint(arg, pltpu.VMEM) for arg in args))


def every(start, stride):
    return pl.ds(start, 8, stride=stride)


def responses(f0, f1, f2, f3, f4):
    n = len(f0)
    forward, back = [], []
    for column in (0, 1):
        ys = []
        for i in range(n):
            if i == 0:
                y = -f0[0] if column == 0 else -f1[0]
            elif i == 1:
                y = -f0[1] * ys[0] - f1[1] if column == 0 else -f0[1] * ys[0]
            else:
                y = -f0[i] * ys[i - 1] - f1[i] * ys[i - 2]
            ys.append(y)
        forward.append(ys)
    for column in (0, 1):
        xs = [None] * n
        for i in reversed(range(n)):
            if i == n - 1:
                x = -f3[i] if column == 0 else -f4[i]
            elif i == n - 2:
                x = -f3[i] * xs[i + 1] - f4[i] if column == 0 else -f3[i] * xs[i + 1]
            else:
                x = -f3[i] * xs[i + 1] - f4[i] * xs[i + 2]
            xs[i] = x
        back.append(xs)
    both = [backward(ys, f2, f3, f4) for ys in forward]
    matrix = [
        forward[0][n - 1], forward[1][n - 1], forward[0][n - 2], forward[1][n - 2],
        back[0][0], back[1][0], back[0][1], back[1][1],
        both[0][0], both[1][0], both[0][1], both[1][1],
    ]
    return back + both, matrix


def backward(ys, f2, f3, f4):
    n = len(ys)
    xs = [None] * n
    for i in reversed(range(n)):
        x = f2[i] * ys[i]
        if i + 1 < n:
            x = x - f3[i] * xs[i + 1]
        if i + 2 < n:
            x = x - f4[i] * xs[i + 2]
        xs[i] = x
    return xs


def solve(vs, f0, f1, f2, f3, f4):
    ys = []
    for i, v in enumerate(vs):
        if i >= 1:
            v = v - f0[i] * ys[i - 1]
        if i >= 2:
            v = v - f1[i] * ys[i - 2]
        ys.append(v)
    xs = backward(ys, f2, f3, f4)
    return xs, (ys[-1], ys[-2], xs[0], xs[1])


def chain(matrices, offsets, first, last):
    n = len(matrices)
    before, after = [], [None] * n
    s1, s2 = first
    for m, o in zip(matrices, offsets):
        before.append((s1, s2))
        n1, n2 = m[0] * s1 + m[1] * s2, m[2] * s1 + m[3] * s2
        s1, s2 = (n1, n2) if o is None else (n1 + o[0], n2 + o[1])
    r1, r2 = last
    for d in reversed(range(n)):
        m, o = matrices[d], offsets[d]
        after[d] = (r1, r2)
        p1, p2 = before[d]
        n1 = m[4] * r1 + m[5] * r2 + (m[8] * p1 + m[9] * p2)
        n2 = m[6] * r1 + m[7] * r2 + (m[10] * p1 + m[11] * p2)
        r1, r2 = (n1, n2) if o is None else (n1 + o[2], n2 + o[3])
    return before, after, (s1, s2), (r1, r2)


def pick(mine, pairs):
    first, second = pairs[0]
    for d in range(1, len(pairs)):
        first = jnp.where(mine == d, pairs[d][0], first)
        second = jnp.where(mine == d, pairs[d][1], second)
    return first, second


def applied(part, response, incoming):
    r1, r2, s1, s2 = incoming
    q1, q2, w1, w2 = response
    return part + (q1 * r1 + q2 * r2) + (w1 * s1 + w2 * s2)


def pack_edges(flow, xi_low, xi_high, eta_low, eta_high):
    lane = lax.broadcasted_iota(jnp.int32, (8, LANES), 1)
    low, high = jnp.zeros((8, LANES), jnp.float32), jnp.zeros((8, LANES), jnp.float32)
    for f in range(5):
        for j in range(2):
            xi_low[2 * f + j] = flow[f, every(j, 8), :]
            xi_high[2 * f + j] = flow[f, every(6 + j, 8), :]
        for z in range(8):
            k = 8 * f + z
            t = flow[f, pl.ds(8 * z, 8), :]
            here = (lane == 2 * k) | (lane == 2 * k + 1)
            low = jnp.where(here, pltpu.roll(t, (2 * k) % LANES, 1), low)
            high = jnp.where(here, pltpu.roll(t, (2 * k + 2) % LANES, 1), high)
    eta_low[...] = low
    eta_high[...] = high


def zeta_responses(flow, fz, qz, message):
    mine = lax.axis_index("zeta")
    for g in range(3):
        rows = [[fz[g, c, pl.ds(8 * z, 8), :] for z in range(8)] for c in range(5)]
        response, matrix = responses(*rows)
        for j in range(4):
            for z in range(8):
                qz[g, j, pl.ds(8 * z, 8), :] = response[j][z]
        for k in range(12):
            for d in range(ZETA):
                message[d, 12 * g + k] = matrix[k]
    for d in range(ZETA):
        place = jnp.where(d > mine, 48, 0)
        for f in range(5):
            for j in range(2):
                message[d, 36 + 2 * f + j] = flow[f, pl.ds(pl.multiple_of(place + 8 * j, 8), 8), :]


def eta_responses(fe, ft, qe, ce, me, turned):
    for p in range(2):
        rows = []
        for c in range(5):
            turned[c] = jnp.concatenate([fe[0, c], fe[1 + p, c]], 0).T
            rows.append([turned[c, every(i, STEPS), :] for i in range(STEPS)])
            for i in range(STEPS):
                ft[p, c, i] = rows[c][i]
        response, matrix = responses(*rows)
        for j in range(4):
            for i in range(STEPS):
                qe[p, j, i] = response[j][i]
        for k in range(12):
            ce[k, every(p, 4), :] = matrix[k]
            ce[k, every(p + 2, 4), :] = matrix[k]
    matrices = [[ce[k, pl.ds(4 * c, 4), :] for k in range(12)] for c in range(CHUNKS)]
    one, zero = jnp.ones((4, LANES), jnp.float32), jnp.zeros((4, LANES), jnp.float32)
    entries = [None] * 12
    for j, unit in enumerate(((one, zero), (zero, one))):
        _, _, (entries[j], entries[2 + j]), (entries[8 + j], entries[10 + j]) = chain(
            matrices, [None] * CHUNKS, unit, (zero, zero)
        )
        _, _, _, (entries[4 + j], entries[6 + j]) = chain(matrices, [None] * CHUNKS, (zero, zero), unit)
    for k in range(12):
        me[pl.ds(4 * k, 4), :] = entries[k]


def xi_responses(fx, qx, message):
    for g in range(3):
        rows = [[fx[g, c, every(x, 8), :] for x in range(8)] for c in range(5)]
        response, matrix = responses(*rows)
        for j in range(4):
            for x in range(8):
                qx[g, j, x] = response[j][x]
        for k in range(12):
            message[every(12 + k if g == 0 else 40 + 2 * k + g - 1, 64), :] = matrix[k]


def zeta_local(residual, flow, fz, xi_prev, xi_next, eta_prev, eta_next, zeta_gathered, part, message, across):
    lane = lax.broadcasted_iota(jnp.int32, (8, LANES), 1)
    zeta, empty = lax.axis_index("zeta"), jnp.zeros((8, LANES), jnp.float32)
    before, after = eta_prev[...], eta_next[...]
    low, high = jnp.maximum(zeta - 1, 0), jnp.minimum(zeta + 1, ZETA - 1)
    for f in range(5):
        xs = [xi_prev[2 * f], xi_prev[2 * f + 1]]
        xs += [flow[f, every(x, 8), :] for x in range(8)]
        xs += [xi_next[2 * f], xi_next[2 * f + 1]]
        for x in range(8):
            across[f, every(x, 8), :] = (
                (xs[x] + xs[x + 4]) - 4.0 * (xs[x + 1] + xs[x + 3]) + 6.0 * xs[x + 2]
            )
        zs = [jnp.where(zeta > 0, zeta_gathered[low, 36 + 2 * f + j], empty) for j in range(2)]
        zs += [flow[f, pl.ds(8 * z, 8), :] for z in range(8)]
        zs += [jnp.where(zeta < ZETA - 1, zeta_gathered[high, 36 + 2 * f + j], empty) for j in range(2)]
        vs = []
        for z in range(8):
            k, t = 8 * f + z, zs[z + 2]
            nxt = pltpu.roll(after, (LANES - 2 * k) % LANES, 1)
            prv = pltpu.roll(before, (LANES - 2 - 2 * k) % LANES, 1)
            up1 = pltpu.roll(jnp.where(lane == 0, nxt, t), LANES - 1, 1)
            up2 = pltpu.roll(jnp.where(lane < 2, nxt, t), LANES - 2, 1)
            down1 = pltpu.roll(jnp.where(lane == LANES - 1, prv, t), 1, 1)
            down2 = pltpu.roll(jnp.where(lane >= LANES - 2, prv, t), 2, 1)
            total = (
                (zs[z] + zs[z + 4] + up2 + down2)
                - 4.0 * (zs[z + 1] + zs[z + 3] + up1 + down1)
                + 12.0 * t
                + across[f, pl.ds(8 * z, 8), :]
            )
            vs.append(residual[f, pl.ds(8 * z, 8), :] - dissipation * total)
        g = field_group[f]
        xs, ends = solve(vs, *[[fz[g, c, pl.ds(8 * z, 8), :] for z in range(8)] for c in range(5)])
        for z in range(8):
            part[f, pl.ds(8 * z, 8), :] = xs[z]
        for v in range(4):
            for d in range(ZETA):
                message[d, 4 * f + v] = ends[v]


def eta_local(part, qz, gathered, matrices, ft, ce, me, epart, ends_of, message, lines, turned):
    mine = lax.axis_index("zeta")
    for f in range(5):
        g = field_group[f]
        before, after, _, _ = chain(
            [[matrices[d, 12 * g + k] for k in range(12)] for d in range(ZETA)],
            [[gathered[d, 4 * f + v] for v in range(4)] for d in range(ZETA)],
            (jnp.zeros((8, LANES), jnp.float32),) * 2,
            (jnp.zeros((8, LANES), jnp.float32),) * 2,
        )
        incoming = pick(mine, after) + pick(mine, before)
        p, half = field_slot[f]
        for z in range(8):
            rows = pl.ds(8 * z, 8)
            lines[p, pl.ds(64 * half + 8 * z, 8), :] = applied(
                part[f, rows, :], [qz[g, j, rows, :] for j in range(4)], incoming
            )
    lines[2, pl.ds(64, 64), :] = jnp.zeros((64, LANES), jnp.float32)
    for p in range(3):
        q = p % 2
        turned[p] = lines[p].T
        vs = [turned[p, every(i, STEPS), :] for i in range(STEPS)]
        xs, ends = solve(vs, *[[ft[q, c, i] for i in range(STEPS)] for c in range(5)])
        for i in range(STEPS):
            epart[p, i] = xs[i]
        for v in range(4):
            ends_of[v, every(p, 4), :] = ends[v]
    zero = jnp.zeros((4, LANES), jnp.float32)
    for v in range(4):
        ends_of[v, every(3, 4), :] = jnp.zeros((8, LANES), jnp.float32)
    _, _, out, back = chain(
        [[ce[k, pl.ds(4 * c, 4), :] for k in range(12)] for c in range(CHUNKS)],
        [[ends_of[v, pl.ds(4 * c, 4), :] for v in range(4)] for c in range(CHUNKS)],
        (zero, zero),
        (zero, zero),
    )
    for d in range(ETA):
        for v, value in enumerate(out + back):
            message[d, pl.ds(4 * v, 4), :] = value
        message[d, pl.ds(16, 48), :] = me[...]


def xi_local(epart, qe, ce, ends_of, gathered, fx, begun, part, message, states, turned, lines):
    mine = lax.axis_index("eta")
    zero = jnp.zeros((4, LANES), jnp.float32)
    before, after, _, _ = chain(
        [[gathered[d, pl.ds(16 + 4 * k, 4), :] for k in range(12)] for d in range(ETA)],
        [[gathered[d, pl.ds(4 * v, 4), :] for v in range(4)] for d in range(ETA)],
        (zero, zero),
        (zero, zero),
    )
    before, after, _, _ = chain(
        [[ce[k, pl.ds(4 * c, 4), :] for k in range(12)] for c in range(CHUNKS)],
        [[ends_of[v, pl.ds(4 * c, 4), :] for v in range(4)] for c in range(CHUNKS)],
        pick(mine, before),
        pick(mine, after),
    )
    for c in range(CHUNKS):
        for v, value in enumerate(after[c] + before[c]):
            states[v, pl.ds(4 * c, 4), :] = value
    for p in range(3):
        q = p % 2
        incoming = [states[v, every(p, 4), :] for v in range(4)]
        for i in range(STEPS):
            turned[p, every(i, STEPS), :] = applied(epart[p, i], [qe[q, j, i] for j in range(4)], incoming)
        lines[p] = turned[p].T
    for f in range(5):
        g = field_group[f]
        p, half = field_slot[f]
        vs = [lines[p, every(64 * half + x, 8), :] for x in range(8)]
        xs, ends = solve(vs, *[[fx[g, c, every(x, 8), :] for x in range(8)] for c in range(5)])
        for x in range(8):
            part[f, x] = xs[x]
        second, place = (0, f) if f < 3 else (1, f - 3)
        for v in range(4):
            message[every(32 * second + 4 * place + v, 64), :] = ends[v]


def xi_lines(gathered, incoming):
    first_row = lax.broadcasted_iota(jnp.int32, (3, LANES), 0) == 0
    zero = jnp.zeros((3, LANES), jnp.float32)

    def row(i):
        return jnp.broadcast_to(gathered[pl.ds(i, 1), :], (3, LANES))

    def lines(entry):
        before, after, _, _ = chain(
            [[entry(32 * d, k) for k in range(12)] for d in range(XI)],
            [[gathered[pl.ds(32 * d + v, 3, stride=4), :] for v in range(4)] for d in range(XI)],
            (zero, zero),
            (zero, zero),
        )
        for d in range(XI):
            for v, value in enumerate(after[d] + before[d]):
                incoming[pl.ds(12 * d + v, 3, stride=4), :] = value

    odd = lax.rem(lax.axis_index("xi"), 2) == 1

    @pl.when(jnp.logical_not(odd))
    def _():
        lines(lambda base, k: row(base + 12 + k))

    @pl.when(odd)
    def _():
        lines(lambda base, k: jnp.where(first_row, row(base + 8 + 2 * k), row(base + 9 + 2 * k)))


def finish(part, qx, incoming, update):
    for f in range(5):
        g = field_group[f]
        second, place = (0, f) if f < 3 else (1, f - 3)
        states = [incoming[every(12 * second + 4 * place + v, 24), :] for v in range(4)]
        for x in range(8):
            update[f, every(x, 8), :] = applied(part[f, x], [qx[g, j, x] for j in range(4)], states)


def shifted(value, axis, count, step):
    return lax.ppermute(value, axis, [(i, i + step) for i in range(count) if 0 <= i + step < count])


def exchange(value, axis):
    return lax.all_to_all(value, axis, 0, 0)


def on_device(residual, flow_state, factors_zeta, factors_eta, factors_xi):
    residual = residual.reshape(5, 64, LANES)
    flow = flow_state.reshape(5, 64, LANES)
    fz, fe, fx = (f.reshape(3, 5, 64, LANES) for f in (factors_zeta, factors_eta, factors_xi))
    qz, message = call(
        zeta_responses, (vmem(3, 4, 64, LANES), vmem(ZETA, 46, 8, LANES)), flow, fz, name="zeta_responses"
    )
    zeta_gathered = exchange(message, "zeta")
    xi_low, xi_high, eta_low, eta_high = call(
        pack_edges, (vmem(10, 8, LANES),) * 2 + (vmem(8, LANES),) * 2, flow, name="pack_edges"
    )
    edges = (
        shifted(xi_high, "xi", XI, 1), shifted(xi_low, "xi", XI, -1),
        shifted(eta_high, "eta", ETA, 1), shifted(eta_low, "eta", ETA, -1),
    )
    part, message = call(
        zeta_local,
        (vmem(5, 64, LANES), vmem(ZETA, 20, 8, LANES)),
        residual, flow, fz, *edges, zeta_gathered,
        scratch=[pltpu.VMEM((5, 64, LANES), jnp.float32)],
        name="zeta_local",
    )
    gathered = exchange(message, "zeta")
    ft, qe, ce, me = call(
        eta_responses,
        (
            vmem(2, 5, STEPS, 8, LANES), vmem(2, 4, STEPS, 8, LANES),
            vmem(12, 32, LANES), vmem(48, LANES),
        ),
        fe,
        scratch=[pltpu.VMEM((5, LANES, LANES), jnp.float32)],
        name="eta_responses",
    )
    qx, begun = call(xi_responses, (vmem(3, 4, 8, 8, LANES), vmem(XI * 32, LANES)), fx, name="xi_responses")
    epart, ends_of, message = call(
        eta_local,
        (vmem(3, STEPS, 8, LANES), vmem(4, 32, LANES), vmem(ETA, 64, LANES)),
        part, qz, gathered, zeta_gathered, ft, ce, me,
        scratch=[pltpu.VMEM((3, LANES, LANES), jnp.float32)] * 2,
        name="eta_local",
    )
    gathered = exchange(message, "eta")
    part, message = call(
        xi_local,
        (vmem(5, 8, 8, LANES), vmem(XI * 32, LANES)),
        epart, qe, ce, ends_of, gathered, fx, begun,
        scratch=[
            pltpu.VMEM((4, 32, LANES), jnp.float32),
            pltpu.VMEM((3, LANES, LANES), jnp.float32),
            pltpu.VMEM((3, LANES, LANES), jnp.float32),
        ],
        aliases={6: 1},
        name="xi_local",
    )
    gathered = exchange(message.reshape(XI, 32, LANES), "xi").reshape(XI * 32, LANES)
    incoming = call(xi_lines, vmem(XI * 12, LANES), gathered, name="xi_lines")
    incoming = exchange(incoming.reshape(XI, 3, 4, LANES), "xi").reshape(XI * 12, LANES)
    update = call(finish, f32(5, 64, LANES), part, qx, incoming, name="finish")
    return update.reshape(5, 8, 8, LANES)


def solution(mesh):
    split = P(None, "zeta", "xi", "eta")
    factor_split = P(None, None, "zeta", "xi", "eta")
    return jax.shard_map(
        on_device,
        mesh=mesh,
        in_specs=(split, split, factor_split, factor_split, factor_split),
        out_specs=split,
        check_vma=False,
    )
```

```python
import jax
import jax.numpy as jnp
from jax import lax
from jax.experimental import pallas as pl
from jax.experimental.pallas import tpu as pltpu
from jax.sharding import PartitionSpec as P

dissipation = 0.05
ZETA, ETA, XI = 4, 8, 16
LANES = 128
field_slot = ((0, 0), (1, 0), (2, 0), (0, 1), (1, 1))
field_group = (0, 0, 0, 1, 2)
CHUNKS = 8
STEPS = LANES // CHUNKS


def f32(*shape):
    return jax.ShapeDtypeStruct(shape, jnp.float32)


def hbm(*shape):
    return pltpu.HBM(shape, jnp.float32)


def vmem(*shape):
    return pltpu.VMEM(shape, jnp.float32)


def call(body, outs, *args, scratch=(), name=None, cost=20000, aliases={}, held=False):
    return pl.pallas_call(
        body,
        out_shape=outs,
        in_specs=[pl.BlockSpec(memory_space=pltpu.HBM if held else pltpu.VMEM)] * len(args),
        out_specs=jax.tree.map(lambda _: pl.BlockSpec(memory_space=pltpu.VMEM), outs),
        scratch_shapes=list(scratch),
        input_output_aliases=aliases,
        name=name,
        cost_estimate=pl.CostEstimate(flops=cost * 1000, bytes_accessed=cost * 100, transcendentals=0),
        compiler_params=pltpu.CompilerParams(vmem_limit_bytes=16 << 20),
    )(*(pltpu.with_memory_space_constraint(arg, pltpu.HBM if held else pltpu.VMEM) for arg in args))


def every(start, stride):
    return pl.ds(start, 8, stride=stride)


def responses(f0, f1, f2, f3, f4):
    n = len(f0)
    forward, back = [], []
    for column in (0, 1):
        ys = []
        for i in range(n):
            if i == 0:
                y = -f0[0] if column == 0 else -f1[0]
            elif i == 1:
                y = -f0[1] * ys[0] - f1[1] if column == 0 else -f0[1] * ys[0]
            else:
                y = -f0[i] * ys[i - 1] - f1[i] * ys[i - 2]
            ys.append(y)
        forward.append(ys)
    for column in (0, 1):
        xs = [None] * n
        for i in reversed(range(n)):
            if i == n - 1:
                x = -f3[i] if column == 0 else -f4[i]
            elif i == n - 2:
                x = -f3[i] * xs[i + 1] - f4[i] if column == 0 else -f3[i] * xs[i + 1]
            else:
                x = -f3[i] * xs[i + 1] - f4[i] * xs[i + 2]
            xs[i] = x
        back.append(xs)
    both = [backward(ys, f2, f3, f4) for ys in forward]
    matrix = [
        forward[0][n - 1], forward[1][n - 1], forward[0][n - 2], forward[1][n - 2],
        back[0][0], back[1][0], back[0][1], back[1][1],
        both[0][0], both[1][0], both[0][1], both[1][1],
    ]
    return back + both, matrix


def backward(ys, f2, f3, f4):
    n = len(ys)
    xs = [None] * n
    for i in reversed(range(n)):
        x = f2[i] * ys[i]
        if i + 1 < n:
            x = x - f3[i] * xs[i + 1]
        if i + 2 < n:
            x = x - f4[i] * xs[i + 2]
        xs[i] = x
    return xs


def solve(vs, f0, f1, f2, f3, f4):
    ys = []
    for i, v in enumerate(vs):
        if i >= 1:
            v = v - f0[i] * ys[i - 1]
        if i >= 2:
            v = v - f1[i] * ys[i - 2]
        ys.append(v)
    xs = backward(ys, f2, f3, f4)
    return xs, (ys[-1], ys[-2], xs[0], xs[1])


def chain(matrices, offsets, first, last):
    n = len(matrices)
    before, after = [], [None] * n
    s1, s2 = first
    for m, o in zip(matrices, offsets):
        before.append((s1, s2))
        n1, n2 = m[0] * s1 + m[1] * s2, m[2] * s1 + m[3] * s2
        s1, s2 = (n1, n2) if o is None else (n1 + o[0], n2 + o[1])
    r1, r2 = last
    for d in reversed(range(n)):
        m, o = matrices[d], offsets[d]
        after[d] = (r1, r2)
        p1, p2 = before[d]
        n1 = m[4] * r1 + m[5] * r2 + (m[8] * p1 + m[9] * p2)
        n2 = m[6] * r1 + m[7] * r2 + (m[10] * p1 + m[11] * p2)
        r1, r2 = (n1, n2) if o is None else (n1 + o[2], n2 + o[3])
    return before, after, (s1, s2), (r1, r2)


def pick(mine, pairs):
    first, second = pairs[0]
    for d in range(1, len(pairs)):
        first = jnp.where(mine == d, pairs[d][0], first)
        second = jnp.where(mine == d, pairs[d][1], second)
    return first, second


def applied(part, response, incoming):
    r1, r2, s1, s2 = incoming
    q1, q2, w1, w2 = response
    return part + (q1 * r1 + q2 * r2) + (w1 * s1 + w2 * s2)


def pack_edges(flow, xi_first, xi_second, eta_low, eta_high):
    xi_odd = lax.rem(lax.axis_index("xi"), 2)
    lane = lax.broadcasted_iota(jnp.int32, (8, LANES), 1)
    low, high = jnp.zeros((8, LANES), jnp.float32), jnp.zeros((8, LANES), jnp.float32)
    for f in range(5):
        for j in range(2):
            before, after = flow[f, every(j, 8), :], flow[f, every(6 + j, 8), :]
            xi_first[2 * f + j] = jnp.where(xi_odd == 1, before, after)
            xi_second[2 * f + j] = jnp.where(xi_odd == 1, after, before)
        for z in range(8):
            k = 8 * f + z
            t = flow[f, pl.ds(8 * z, 8), :]
            here = (lane == 2 * k) | (lane == 2 * k + 1)
            low = jnp.where(here, pltpu.roll(t, (2 * k) % LANES, 1), low)
            high = jnp.where(here, pltpu.roll(t, (2 * k + 2) % LANES, 1), high)
    eta_low[...] = low
    eta_high[...] = high


def zeta_responses(flow_held, fz_held, qz, message, flow, fz, arrived):
    copies = [pltpu.make_async_copy(fz_held.at[g], fz.at[g], arrived.at[g]) for g in range(3)]
    copies.append(pltpu.make_async_copy(flow_held, flow, arrived.at[3]))
    for copy in copies:
        copy.start()
    mine = lax.axis_index("zeta")
    for g in range(3):
        copies[g].wait()
        rows = [[fz[g, c, pl.ds(8 * z, 8), :] for z in range(8)] for c in range(5)]
        response, matrix = responses(*rows)
        for j in range(4):
            for z in range(8):
                qz[g, j, pl.ds(8 * z, 8), :] = response[j][z]
        for k in range(12):
            for d in range(ZETA):
                message[d, 12 * g + k] = matrix[k]
    copies[3].wait()
    for d in range(ZETA):
        place = jnp.where(d > mine, 48, 0)
        for f in range(5):
            for j in range(2):
                message[d, 36 + 2 * f + j] = flow[f, pl.ds(pl.multiple_of(place + 8 * j, 8), 8), :]


def eta_responses(fe, ft, qe, ce, me, turned):
    for p in range(2):
        rows = []
        for c in range(5):
            turned[c] = jnp.concatenate([fe[0, c], fe[1 + p, c]], 0).T
            rows.append([turned[c, every(i, STEPS), :] for i in range(STEPS)])
            for i in range(STEPS):
                ft[p, c, i] = rows[c][i]
        response, matrix = responses(*rows)
        for j in range(4):
            for i in range(STEPS):
                qe[p, j, i] = response[j][i]
        for k in range(12):
            ce[k, every(p, 4), :] = matrix[k]
            ce[k, every(p + 2, 4), :] = matrix[k]
    matrices = [[ce[k, pl.ds(4 * c, 4), :] for k in range(12)] for c in range(CHUNKS)]
    one, zero = jnp.ones((4, LANES), jnp.float32), jnp.zeros((4, LANES), jnp.float32)
    entries = [None] * 12
    for j, unit in enumerate(((one, zero), (zero, one))):
        _, _, (entries[j], entries[2 + j]), (entries[8 + j], entries[10 + j]) = chain(
            matrices, [None] * CHUNKS, unit, (zero, zero)
        )
        _, _, _, (entries[4 + j], entries[6 + j]) = chain(matrices, [None] * CHUNKS, (zero, zero), unit)
    for k in range(12):
        me[pl.ds(4 * k, 4), :] = entries[k]


def xi_responses(fx, qx, message):
    for g in range(3):
        rows = [[fx[g, c, every(x, 8), :] for x in range(8)] for c in range(5)]
        response, matrix = responses(*rows)
        for j in range(4):
            for x in range(8):
                qx[g, j, x] = response[j][x]
        for k in range(12):
            message[every(12 + k if g == 0 else 40 + 2 * k + g - 1, 64), :] = matrix[k]


def zeta_local(residual, flow, fz, xi_first, xi_second, eta_prev, eta_next, zeta_gathered, _, __, part, message, across):
    lane = lax.broadcasted_iota(jnp.int32, (8, LANES), 1)
    zeta, empty = lax.axis_index("zeta"), jnp.zeros((8, LANES), jnp.float32)
    xi_odd, eta = lax.rem(lax.axis_index("xi"), 2) == 1, lax.axis_index("eta")
    before = jnp.where(eta > 0, eta_prev[...], empty)
    after = jnp.where(eta < ETA - 1, eta_next[...], empty)
    low, high = jnp.maximum(zeta - 1, 0), jnp.minimum(zeta + 1, ZETA - 1)
    for f in range(5):
        xs = [jnp.where(xi_odd, xi_first[2 * f + j], xi_second[2 * f + j]) for j in range(2)]
        xs += [flow[f, every(x, 8), :] for x in range(8)]
        xs += [jnp.where(xi_odd, xi_second[2 * f + j], xi_first[2 * f + j]) for j in range(2)]
        for x in range(8):
            across[f, every(x, 8), :] = (
                (xs[x] + xs[x + 4]) - 4.0 * (xs[x + 1] + xs[x + 3]) + 6.0 * xs[x + 2]
            )
        zs = [jnp.where(zeta > 0, zeta_gathered[low, 36 + 2 * f + j], empty) for j in range(2)]
        zs += [flow[f, pl.ds(8 * z, 8), :] for z in range(8)]
        zs += [jnp.where(zeta < ZETA - 1, zeta_gathered[high, 36 + 2 * f + j], empty) for j in range(2)]
        vs = []
        for z in range(8):
            k, t = 8 * f + z, zs[z + 2]
            nxt = pltpu.roll(after, (LANES - 2 * k) % LANES, 1)
            prv = pltpu.roll(before, (LANES - 2 - 2 * k) % LANES, 1)
            up1 = pltpu.roll(jnp.where(lane == 0, nxt, t), LANES - 1, 1)
            up2 = pltpu.roll(jnp.where(lane < 2, nxt, t), LANES - 2, 1)
            down1 = pltpu.roll(jnp.where(lane == LANES - 1, prv, t), 1, 1)
            down2 = pltpu.roll(jnp.where(lane >= LANES - 2, prv, t), 2, 1)
            total = (
                (zs[z] + zs[z + 4] + up2 + down2)
                - 4.0 * (zs[z + 1] + zs[z + 3] + up1 + down1)
                + 12.0 * t
                + across[f, pl.ds(8 * z, 8), :]
            )
            vs.append(residual[f, pl.ds(8 * z, 8), :] - dissipation * total)
        g = field_group[f]
        xs, ends = solve(vs, *[[fz[g, c, pl.ds(8 * z, 8), :] for z in range(8)] for c in range(5)])
        for z in range(8):
            part[f, pl.ds(8 * z, 8), :] = xs[z]
        for v in range(4):
            for d in range(ZETA):
                message[d, 4 * f + v] = ends[v]


def eta_local(part, qz, gathered, matrices, ft, ce, me, epart, ends_of, message, lines, turned):
    mine = lax.axis_index("zeta")
    for f in range(5):
        g = field_group[f]
        before, after, _, _ = chain(
            [[matrices[d, 12 * g + k] for k in range(12)] for d in range(ZETA)],
            [[gathered[d, 4 * f + v] for v in range(4)] for d in range(ZETA)],
            (jnp.zeros((8, LANES), jnp.float32),) * 2,
            (jnp.zeros((8, LANES), jnp.float32),) * 2,
        )
        incoming = pick(mine, after) + pick(mine, before)
        p, half = field_slot[f]
        for z in range(8):
            rows = pl.ds(8 * z, 8)
            lines[p, pl.ds(64 * half + 8 * z, 8), :] = applied(
                part[f, rows, :], [qz[g, j, rows, :] for j in range(4)], incoming
            )
    lines[2, pl.ds(64, 64), :] = jnp.zeros((64, LANES), jnp.float32)
    for p in range(3):
        q = p % 2
        turned[p] = lines[p].T
        vs = [turned[p, every(i, STEPS), :] for i in range(STEPS)]
        xs, ends = solve(vs, *[[ft[q, c, i] for i in range(STEPS)] for c in range(5)])
        for i in range(STEPS):
            epart[p, i] = xs[i]
        for v in range(4):
            ends_of[v, every(p, 4), :] = ends[v]
    zero = jnp.zeros((4, LANES), jnp.float32)
    for v in range(4):
        ends_of[v, every(3, 4), :] = jnp.zeros((8, LANES), jnp.float32)
    _, _, out, back = chain(
        [[ce[k, pl.ds(4 * c, 4), :] for k in range(12)] for c in range(CHUNKS)],
        [[ends_of[v, pl.ds(4 * c, 4), :] for v in range(4)] for c in range(CHUNKS)],
        (zero, zero),
        (zero, zero),
    )
    for d in range(ETA):
        for v, value in enumerate(out + back):
            message[d, pl.ds(4 * v, 4), :] = value
        message[d, pl.ds(16, 48), :] = me[...]


def xi_local(epart, qe, ce, ends_of, gathered, fx, begun, part, message, states, turned, lines):
    mine = lax.axis_index("eta")
    zero = jnp.zeros((4, LANES), jnp.float32)
    before, after, _, _ = chain(
        [[gathered[d, pl.ds(16 + 4 * k, 4), :] for k in range(12)] for d in range(ETA)],
        [[gathered[d, pl.ds(4 * v, 4), :] for v in range(4)] for d in range(ETA)],
        (zero, zero),
        (zero, zero),
    )
    before, after, _, _ = chain(
        [[ce[k, pl.ds(4 * c, 4), :] for k in range(12)] for c in range(CHUNKS)],
        [[ends_of[v, pl.ds(4 * c, 4), :] for v in range(4)] for c in range(CHUNKS)],
        pick(mine, before),
        pick(mine, after),
    )
    for c in range(CHUNKS):
        for v, value in enumerate(after[c] + before[c]):
            states[v, pl.ds(4 * c, 4), :] = value
    for p in range(3):
        q = p % 2
        incoming = [states[v, every(p, 4), :] for v in range(4)]
        for i in range(STEPS):
            turned[p, every(i, STEPS), :] = applied(epart[p, i], [qe[q, j, i] for j in range(4)], incoming)
        lines[p] = turned[p].T
    for f in range(5):
        g = field_group[f]
        p, half = field_slot[f]
        vs = [lines[p, every(64 * half + x, 8), :] for x in range(8)]
        xs, ends = solve(vs, *[[fx[g, c, every(x, 8), :] for x in range(8)] for c in range(5)])
        for x in range(8):
            part[f, x] = xs[x]
        second, place = (0, f) if f < 3 else (1, f - 3)
        for v in range(4):
            message[every(32 * second + 4 * place + v, 64), :] = ends[v]


def xi_lines(gathered, incoming):
    first_row = lax.broadcasted_iota(jnp.int32, (3, LANES), 0) == 0
    zero = jnp.zeros((3, LANES), jnp.float32)

    def row(i):
        return jnp.broadcast_to(gathered[pl.ds(i, 1), :], (3, LANES))

    def lines(entry):
        before, after, _, _ = chain(
            [[entry(32 * d, k) for k in range(12)] for d in range(XI)],
            [[gathered[pl.ds(32 * d + v, 3, stride=4), :] for v in range(4)] for d in range(XI)],
            (zero, zero),
            (zero, zero),
        )
        for d in range(XI):
            for v, value in enumerate(after[d] + before[d]):
                incoming[pl.ds(12 * d + v, 3, stride=4), :] = value

    odd = lax.rem(lax.axis_index("xi"), 2) == 1

    @pl.when(jnp.logical_not(odd))
    def _():
        lines(lambda base, k: row(base + 12 + k))

    @pl.when(odd)
    def _():
        lines(lambda base, k: jnp.where(first_row, row(base + 8 + 2 * k), row(base + 9 + 2 * k)))


def finish(part, qx, incoming, update):
    for f in range(5):
        g = field_group[f]
        second, place = (0, f) if f < 3 else (1, f - 3)
        states = [incoming[every(12 * second + 4 * place + v, 24), :] for v in range(4)]
        for x in range(8):
            update[f, every(x, 8), :] = applied(part[f, x], [qx[g, j, x] for j in range(4)], states)


def swapped(value, axis, count, start):
    pairs = [(i, i + 1) for i in range(start, count - 1, 2)]
    return lax.ppermute(value, axis, pairs + [(j, i) for i, j in pairs])


def around(value, axis, count, step):
    return lax.ppermute(value, axis, [(i, (i + step) % count) for i in range(count)])


def exchange(value, axis):
    return lax.all_to_all(value, axis, 0, 0)


def on_device(residual, flow_state, factors_zeta, factors_eta, factors_xi):
    residual = residual.reshape(5, 64, LANES)
    flow = flow_state.reshape(5, 64, LANES)
    fz, fe, fx = (f.reshape(3, 5, 64, LANES) for f in (factors_zeta, factors_eta, factors_xi))
    qz, message = call(
        zeta_responses,
        (hbm(3, 4, 64, LANES), vmem(ZETA, 46, 8, LANES)),
        flow, fz,
        scratch=[vmem(5, 64, LANES), vmem(3, 5, 64, LANES), pltpu.SemaphoreType.DMA((4,))],
        held=True,
        name="zeta_responses",
    )
    zeta_gathered = exchange(message, "zeta")
    xi_first, xi_second, eta_low, eta_high = call(
        pack_edges, (vmem(10, 8, LANES),) * 2 + (vmem(8, LANES),) * 2, flow, name="pack_edges"
    )
    edges = (
        swapped(xi_first, "xi", XI, 0), swapped(xi_second, "xi", XI, 1),
        around(eta_high, "eta", ETA, 1), around(eta_low, "eta", ETA, -1),
    )
    ft, qe, ce, me = call(
        eta_responses,
        (
            hbm(2, 5, STEPS, 8, LANES), hbm(2, 4, STEPS, 8, LANES),
            vmem(12, 32, LANES), vmem(48, LANES),
        ),
        fe,
        scratch=[pltpu.VMEM((5, LANES, LANES), jnp.float32)],
        name="eta_responses",
    )
    qx, begun = call(xi_responses, (hbm(3, 4, 8, 8, LANES), vmem(XI * 32, LANES)), fx, name="xi_responses")
    part, message = call(
        zeta_local,
        (vmem(5, 64, LANES), vmem(ZETA, 20, 8, LANES)),
        residual, flow, fz, *edges, zeta_gathered, ce, begun,
        scratch=[pltpu.VMEM((5, 64, LANES), jnp.float32)],
        name="zeta_local",
    )
    gathered = exchange(message, "zeta")
    epart, ends_of, message = call(
        eta_local,
        (vmem(3, STEPS, 8, LANES), vmem(4, 32, LANES), vmem(ETA, 64, LANES)),
        part, qz, gathered, zeta_gathered, ft, ce, me,
        scratch=[pltpu.VMEM((3, LANES, LANES), jnp.float32)] * 2,
        name="eta_local",
    )
    gathered = exchange(message, "eta")
    part, message = call(
        xi_local,
        (vmem(5, 8, 8, LANES), vmem(XI * 32, LANES)),
        epart, qe, ce, ends_of, gathered, fx, begun,
        scratch=[
            pltpu.VMEM((4, 32, LANES), jnp.float32),
            pltpu.VMEM((3, LANES, LANES), jnp.float32),
            pltpu.VMEM((3, LANES, LANES), jnp.float32),
        ],
        aliases={6: 1},
        name="xi_local",
    )
    gathered = exchange(message.reshape(XI, 32, LANES), "xi").reshape(XI * 32, LANES)
    incoming = call(xi_lines, vmem(XI * 12, LANES), gathered, name="xi_lines")
    incoming = exchange(incoming.reshape(XI, 3, 4, LANES), "xi").reshape(XI * 12, LANES)
    update = call(finish, f32(5, 64, LANES), part, qx, incoming, name="finish")
    return update.reshape(5, 8, 8, LANES)


def solution(mesh):
    split = P(None, "zeta", "xi", "eta")
    factor_split = P(None, None, "zeta", "xi", "eta")
    return jax.shard_map(
        on_device,
        mesh=mesh,
        in_specs=(split, split, factor_split, factor_split, factor_split),
        out_specs=split,
        check_vma=False,
    )
```

```python
import jax
import jax.numpy as jnp
from jax import lax
from jax.experimental import pallas as pl
from jax.experimental.pallas import tpu as pltpu
from jax.sharding import PartitionSpec as P

dissipation = 0.05
ZETA, ETA, XI = 4, 8, 16
LANES = 128
field_slot = ((0, 0), (1, 0), (2, 0), (0, 1), (1, 1))
field_group = (0, 0, 0, 1, 2)
CHUNKS = 8
STEPS = LANES // CHUNKS


def f32(*shape):
    return jax.ShapeDtypeStruct(shape, jnp.float32)


def hbm(*shape):
    return pltpu.HBM(shape, jnp.float32)


def vmem(*shape):
    return pltpu.VMEM(shape, jnp.float32)


def call(body, outs, *args, scratch=(), name=None, cost=20000, aliases={}, held=False):
    return pl.pallas_call(
        body,
        out_shape=outs,
        in_specs=[pl.BlockSpec(memory_space=pltpu.HBM if held else pltpu.VMEM)] * len(args),
        out_specs=jax.tree.map(lambda _: pl.BlockSpec(memory_space=pltpu.VMEM), outs),
        scratch_shapes=list(scratch),
        input_output_aliases=aliases,
        name=name,
        cost_estimate=pl.CostEstimate(flops=cost * 1000, bytes_accessed=cost * 100, transcendentals=0),
        compiler_params=pltpu.CompilerParams(vmem_limit_bytes=16 << 20),
    )(*(pltpu.with_memory_space_constraint(arg, pltpu.HBM if held else pltpu.VMEM) for arg in args))


def every(start, stride):
    return pl.ds(start, 8, stride=stride)


def responses(f0, f1, f2, f3, f4):
    n = len(f0)
    forward, back = [], []
    for column in (0, 1):
        ys = []
        for i in range(n):
            if i == 0:
                y = -f0[0] if column == 0 else -f1[0]
            elif i == 1:
                y = -f0[1] * ys[0] - f1[1] if column == 0 else -f0[1] * ys[0]
            else:
                y = -f0[i] * ys[i - 1] - f1[i] * ys[i - 2]
            ys.append(y)
        forward.append(ys)
    for column in (0, 1):
        xs = [None] * n
        for i in reversed(range(n)):
            if i == n - 1:
                x = -f3[i] if column == 0 else -f4[i]
            elif i == n - 2:
                x = -f3[i] * xs[i + 1] - f4[i] if column == 0 else -f3[i] * xs[i + 1]
            else:
                x = -f3[i] * xs[i + 1] - f4[i] * xs[i + 2]
            xs[i] = x
        back.append(xs)
    both = [backward(ys, f2, f3, f4) for ys in forward]
    matrix = [
        forward[0][n - 1], forward[1][n - 1], forward[0][n - 2], forward[1][n - 2],
        back[0][0], back[1][0], back[0][1], back[1][1],
        both[0][0], both[1][0], both[0][1], both[1][1],
    ]
    return back + both, matrix


def backward(ys, f2, f3, f4):
    n = len(ys)
    xs = [None] * n
    for i in reversed(range(n)):
        x = f2[i] * ys[i]
        if i + 1 < n:
            x = x - f3[i] * xs[i + 1]
        if i + 2 < n:
            x = x - f4[i] * xs[i + 2]
        xs[i] = x
    return xs


def solve(vs, f0, f1, f2, f3, f4):
    ys = []
    for i, v in enumerate(vs):
        if i >= 1:
            v = v - f0[i] * ys[i - 1]
        if i >= 2:
            v = v - f1[i] * ys[i - 2]
        ys.append(v)
    xs = backward(ys, f2, f3, f4)
    return xs, (ys[-1], ys[-2], xs[0], xs[1])


def chain(matrices, offsets, first, last):
    n = len(matrices)
    before, after = [], [None] * n
    s1, s2 = first
    for m, o in zip(matrices, offsets):
        before.append((s1, s2))
        n1, n2 = m[0] * s1 + m[1] * s2, m[2] * s1 + m[3] * s2
        s1, s2 = (n1, n2) if o is None else (n1 + o[0], n2 + o[1])
    r1, r2 = last
    for d in reversed(range(n)):
        m, o = matrices[d], offsets[d]
        after[d] = (r1, r2)
        p1, p2 = before[d]
        n1 = m[4] * r1 + m[5] * r2 + (m[8] * p1 + m[9] * p2)
        n2 = m[6] * r1 + m[7] * r2 + (m[10] * p1 + m[11] * p2)
        r1, r2 = (n1, n2) if o is None else (n1 + o[2], n2 + o[3])
    return before, after, (s1, s2), (r1, r2)


def pick(mine, pairs):
    first, second = pairs[0]
    for d in range(1, len(pairs)):
        first = jnp.where(mine == d, pairs[d][0], first)
        second = jnp.where(mine == d, pairs[d][1], second)
    return first, second


def applied(part, response, incoming):
    r1, r2, s1, s2 = incoming
    q1, q2, w1, w2 = response
    return part + (q1 * r1 + q2 * r2) + (w1 * s1 + w2 * s2)


def pack_edges(flow, xi_first, xi_second, eta_low, eta_high):
    xi_odd = lax.rem(lax.axis_index("xi"), 2)
    lane = lax.broadcasted_iota(jnp.int32, (8, LANES), 1)
    low, high = jnp.zeros((8, LANES), jnp.float32), jnp.zeros((8, LANES), jnp.float32)
    for f in range(5):
        for j in range(2):
            before, after = flow[f, every(j, 8), :], flow[f, every(6 + j, 8), :]
            xi_first[2 * f + j] = jnp.where(xi_odd == 1, before, after)
            xi_second[2 * f + j] = jnp.where(xi_odd == 1, after, before)
        for z in range(8):
            k = 8 * f + z
            t = flow[f, pl.ds(8 * z, 8), :]
            here = (lane == 2 * k) | (lane == 2 * k + 1)
            low = jnp.where(here, pltpu.roll(t, (2 * k) % LANES, 1), low)
            high = jnp.where(here, pltpu.roll(t, (2 * k + 2) % LANES, 1), high)
    eta_low[...] = low
    eta_high[...] = high


def zeta_responses(flow_held, fz_held, qz, message, flow, fz, arrived):
    copies = [pltpu.make_async_copy(fz_held.at[g], fz.at[g], arrived.at[g]) for g in range(3)]
    copies.append(pltpu.make_async_copy(flow_held, flow, arrived.at[3]))
    for copy in copies:
        copy.start()
    mine = lax.axis_index("zeta")
    for g in range(3):
        copies[g].wait()
        rows = [[fz[g, c, pl.ds(8 * z, 8), :] for z in range(8)] for c in range(5)]
        response, matrix = responses(*rows)
        for j in range(4):
            for z in range(8):
                qz[g, j, pl.ds(8 * z, 8), :] = response[j][z]
        for k in range(12):
            for d in range(ZETA):
                message[d, 12 * g + k] = matrix[k]
    copies[3].wait()
    for d in range(ZETA):
        place = jnp.where(d > mine, 48, 0)
        for f in range(5):
            for j in range(2):
                message[d, 36 + 2 * f + j] = flow[f, pl.ds(pl.multiple_of(place + 8 * j, 8), 8), :]


def eta_responses(fe, ft, qe, ce, me, turned):
    for p in range(2):
        rows = []
        for c in range(5):
            turned[c] = jnp.concatenate([fe[0, c], fe[1 + p, c]], 0).T
            rows.append([turned[c, every(i, STEPS), :] for i in range(STEPS)])
            for i in range(STEPS):
                ft[p, c, i] = rows[c][i]
        response, matrix = responses(*rows)
        for j in range(4):
            for i in range(STEPS):
                qe[p, j, i] = response[j][i]
        for k in range(12):
            ce[k, every(p, 4), :] = matrix[k]
            ce[k, every(p + 2, 4), :] = matrix[k]
    matrices = [[ce[k, pl.ds(4 * c, 4), :] for k in range(12)] for c in range(CHUNKS)]
    one, zero = jnp.ones((4, LANES), jnp.float32), jnp.zeros((4, LANES), jnp.float32)
    entries = [None] * 12
    for j, unit in enumerate(((one, zero), (zero, one))):
        _, _, (entries[j], entries[2 + j]), (entries[8 + j], entries[10 + j]) = chain(
            matrices, [None] * CHUNKS, unit, (zero, zero)
        )
        _, _, _, (entries[4 + j], entries[6 + j]) = chain(matrices, [None] * CHUNKS, (zero, zero), unit)
    for k in range(12):
        me[pl.ds(2 * k, 2), :] = entries[k][0:2]


def put_halves(message, row, left, right):
    low = lax.broadcasted_iota(jnp.int32, (8, LANES), 1) < 64
    message[every(row, 56), :] = jnp.where(low, left, pltpu.roll(right, 64, 1))
    message[every(28 + row, 56), :] = jnp.where(low, pltpu.roll(left, 64, 1), right)


def xi_responses(fx, qx, message):
    matrices = []
    for g in range(3):
        rows = [[fx[g, c, every(x, 8), :] for x in range(8)] for c in range(5)]
        response, matrix = responses(*rows)
        matrices.append(matrix)
        for j in range(4):
            for x in range(8):
                qx[g, j, x] = response[j][x]
    for k in range(12):
        put_halves(message, k, matrices[0][k], matrices[1][k])
    for k in range(6):
        put_halves(message, 12 + k, matrices[2][k], matrices[2][k + 6])


def zeta_local(residual, flow, fz, xi_first, xi_second, eta_prev, eta_next, zeta_gathered, _, __, part, message, across):
    lane = lax.broadcasted_iota(jnp.int32, (8, LANES), 1)
    zeta, empty = lax.axis_index("zeta"), jnp.zeros((8, LANES), jnp.float32)
    xi_odd, eta = lax.rem(lax.axis_index("xi"), 2) == 1, lax.axis_index("eta")
    before = jnp.where(eta > 0, eta_prev[...], empty)
    after = jnp.where(eta < ETA - 1, eta_next[...], empty)
    low, high = jnp.maximum(zeta - 1, 0), jnp.minimum(zeta + 1, ZETA - 1)
    for f in range(5):
        xs = [jnp.where(xi_odd, xi_first[2 * f + j], xi_second[2 * f + j]) for j in range(2)]
        xs += [flow[f, every(x, 8), :] for x in range(8)]
        xs += [jnp.where(xi_odd, xi_second[2 * f + j], xi_first[2 * f + j]) for j in range(2)]
        for x in range(8):
            across[f, every(x, 8), :] = (
                (xs[x] + xs[x + 4]) - 4.0 * (xs[x + 1] + xs[x + 3]) + 6.0 * xs[x + 2]
            )
        zs = [jnp.where(zeta > 0, zeta_gathered[low, 36 + 2 * f + j], empty) for j in range(2)]
        zs += [flow[f, pl.ds(8 * z, 8), :] for z in range(8)]
        zs += [jnp.where(zeta < ZETA - 1, zeta_gathered[high, 36 + 2 * f + j], empty) for j in range(2)]
        vs = []
        for z in range(8):
            k, t = 8 * f + z, zs[z + 2]
            nxt = pltpu.roll(after, (LANES - 2 * k) % LANES, 1)
            prv = pltpu.roll(before, (LANES - 2 - 2 * k) % LANES, 1)
            up1 = pltpu.roll(jnp.where(lane == 0, nxt, t), LANES - 1, 1)
            up2 = pltpu.roll(jnp.where(lane < 2, nxt, t), LANES - 2, 1)
            down1 = pltpu.roll(jnp.where(lane == LANES - 1, prv, t), 1, 1)
            down2 = pltpu.roll(jnp.where(lane >= LANES - 2, prv, t), 2, 1)
            total = (
                (zs[z] + zs[z + 4] + up2 + down2)
                - 4.0 * (zs[z + 1] + zs[z + 3] + up1 + down1)
                + 12.0 * t
                + across[f, pl.ds(8 * z, 8), :]
            )
            vs.append(residual[f, pl.ds(8 * z, 8), :] - dissipation * total)
        g = field_group[f]
        xs, ends = solve(vs, *[[fz[g, c, pl.ds(8 * z, 8), :] for z in range(8)] for c in range(5)])
        for z in range(8):
            part[f, pl.ds(8 * z, 8), :] = xs[z]
        for v in range(4):
            for d in range(ZETA):
                message[d, 4 * f + v] = ends[v]


def eta_local(part, qz, gathered, matrices, ft, ce, me, epart, ends_of, message, lines, turned):
    mine = lax.axis_index("zeta")
    for f in range(5):
        g = field_group[f]
        before, after, _, _ = chain(
            [[matrices[d, 12 * g + k] for k in range(12)] for d in range(ZETA)],
            [[gathered[d, 4 * f + v] for v in range(4)] for d in range(ZETA)],
            (jnp.zeros((8, LANES), jnp.float32),) * 2,
            (jnp.zeros((8, LANES), jnp.float32),) * 2,
        )
        incoming = pick(mine, after) + pick(mine, before)
        p, half = field_slot[f]
        for z in range(8):
            rows = pl.ds(8 * z, 8)
            lines[p, pl.ds(64 * half + 8 * z, 8), :] = applied(
                part[f, rows, :], [qz[g, j, rows, :] for j in range(4)], incoming
            )
    lines[2, pl.ds(64, 64), :] = jnp.zeros((64, LANES), jnp.float32)
    for p in range(3):
        q = p % 2
        turned[p] = lines[p].T
        vs = [turned[p, every(i, STEPS), :] for i in range(STEPS)]
        xs, ends = solve(vs, *[[ft[q, c, i] for i in range(STEPS)] for c in range(5)])
        for i in range(STEPS):
            epart[p, i] = xs[i]
        for v in range(4):
            ends_of[v, every(p, 4), :] = ends[v]
    zero = jnp.zeros((4, LANES), jnp.float32)
    for v in range(4):
        ends_of[v, every(3, 4), :] = jnp.zeros((8, LANES), jnp.float32)
    _, _, out, back = chain(
        [[ce[k, pl.ds(4 * c, 4), :] for k in range(12)] for c in range(CHUNKS)],
        [[ends_of[v, pl.ds(4 * c, 4), :] for v in range(4)] for c in range(CHUNKS)],
        (zero, zero),
        (zero, zero),
    )
    for d in range(ETA):
        for v, value in enumerate(out + back):
            message[d, pl.ds(4 * v, 4), :] = value
        message[d, pl.ds(16, 24), :] = me[...]


def xi_local(epart, qe, ce, ends_of, gathered, fx, begun, part, message, states, turned, lines):
    mine = lax.axis_index("eta")
    zero = jnp.zeros((4, LANES), jnp.float32)
    odd_row = lax.rem(lax.broadcasted_iota(jnp.int32, (4, LANES), 0), 2) == 1

    def entry(d, k):
        even, odd = (jnp.broadcast_to(gathered[d, pl.ds(16 + 2 * k + i, 1), :], (4, LANES)) for i in (0, 1))
        return jnp.where(odd_row, odd, even)

    before, after, _, _ = chain(
        [[entry(d, k) for k in range(12)] for d in range(ETA)],
        [[gathered[d, pl.ds(4 * v, 4), :] for v in range(4)] for d in range(ETA)],
        (zero, zero),
        (zero, zero),
    )
    before, after, _, _ = chain(
        [[ce[k, pl.ds(4 * c, 4), :] for k in range(12)] for c in range(CHUNKS)],
        [[ends_of[v, pl.ds(4 * c, 4), :] for v in range(4)] for c in range(CHUNKS)],
        pick(mine, before),
        pick(mine, after),
    )
    for c in range(CHUNKS):
        for v, value in enumerate(after[c] + before[c]):
            states[v, pl.ds(4 * c, 4), :] = value
    for p in range(3):
        q = p % 2
        incoming = [states[v, every(p, 4), :] for v in range(4)]
        for i in range(STEPS):
            turned[p, every(i, STEPS), :] = applied(epart[p, i], [qe[q, j, i] for j in range(4)], incoming)
        lines[p] = turned[p].T
    all_ends = []
    for f in range(5):
        g = field_group[f]
        p, half = field_slot[f]
        vs = [lines[p, every(64 * half + x, 8), :] for x in range(8)]
        xs, ends = solve(vs, *[[fx[g, c, every(x, 8), :] for x in range(8)] for c in range(5)])
        for x in range(8):
            part[f, x] = xs[x]
        all_ends.append(ends)
    for v in range(4):
        put_halves(message, 18 + v, all_ends[0][v], all_ends[3][v])
        put_halves(message, 22 + v, all_ends[1][v], all_ends[4][v])
    for v in range(2):
        put_halves(message, 26 + v, all_ends[2][v], all_ends[2][v + 2])


def xi_lines(gathered, incoming, turned):
    row = lax.broadcasted_iota(jnp.int32, (3, LANES), 0)
    upper = lax.broadcasted_iota(jnp.int32, (3, LANES), 1) >= 64
    for d in range(XI):
        turned[pl.ds(8 * d, 6), :] = pltpu.roll(gathered[pl.ds(28 * d + 12, 6), :], 64, 1)
        turned[pl.ds(8 * d + 6, 2), :] = pltpu.roll(gathered[pl.ds(28 * d + 26, 2), :], 64, 1)

    def spread(ref, i):
        return jnp.broadcast_to(ref[pl.ds(i, 1), :], (3, LANES))

    def entry(d, k):
        other = spread(turned, 8 * d + k) if k < 6 else spread(gathered, 28 * d + 6 + k)
        return jnp.where((row == 1) & upper, other, spread(gathered, 28 * d + k))

    def offset(d, v):
        if v < 2:
            return gathered[pl.ds(28 * d + 18 + v, 3, stride=4), :]
        last = spread(turned, 8 * d + 4 + v)
        first, second = spread(gathered, 28 * d + 18 + v), spread(gathered, 28 * d + 22 + v)
        return jnp.where(row == 0, first, jnp.where(row == 1, second, last))

    zero = jnp.zeros((3, LANES), jnp.float32)
    before, after, _, _ = chain(
        [[entry(d, k) for k in range(12)] for d in range(XI)],
        [[offset(d, v) for v in range(4)] for d in range(XI)],
        (zero, zero),
        (zero, zero),
    )
    for d in range(XI):
        for v, value in enumerate(after[d] + before[d]):
            incoming[pl.ds(12 * d + v, 3, stride=4), :] = value


def finish(part, qx, incoming, update):
    low = lax.broadcasted_iota(jnp.int32, (8, LANES), 1) < 64
    for f in range(5):
        g = field_group[f]
        p, half = field_slot[f]
        states = []
        for v in range(4):
            near, far = incoming[every(4 * p + v, 24), :], incoming[every(12 + 4 * p + v, 24), :]
            if half == 0:
                states.append(jnp.where(low, near, pltpu.roll(far, 64, 1)))
            else:
                states.append(jnp.where(low, pltpu.roll(near, 64, 1), far))
        for x in range(8):
            update[f, every(x, 8), :] = applied(part[f, x], [qx[g, j, x] for j in range(4)], states)


def swapped(value, axis, count, start):
    pairs = [(i, i + 1) for i in range(start, count - 1, 2)]
    return lax.ppermute(value, axis, pairs + [(j, i) for i, j in pairs])


def around(value, axis, count, step):
    return lax.ppermute(value, axis, [(i, (i + step) % count) for i in range(count)])


def exchange(value, axis):
    return lax.all_to_all(value, axis, 0, 0)


def on_device(residual, flow_state, factors_zeta, factors_eta, factors_xi):
    residual = residual.reshape(5, 64, LANES)
    flow = flow_state.reshape(5, 64, LANES)
    fz, fe, fx = (f.reshape(3, 5, 64, LANES) for f in (factors_zeta, factors_eta, factors_xi))
    qz, message = call(
        zeta_responses,
        (hbm(3, 4, 64, LANES), vmem(ZETA, 46, 8, LANES)),
        flow, fz,
        scratch=[vmem(5, 64, LANES), vmem(3, 5, 64, LANES), pltpu.SemaphoreType.DMA((4,))],
        held=True,
        name="zeta_responses",
    )
    zeta_gathered = exchange(message, "zeta")
    xi_first, xi_second, eta_low, eta_high = call(
        pack_edges, (vmem(10, 8, LANES),) * 2 + (vmem(8, LANES),) * 2, flow, name="pack_edges"
    )
    edges = (
        swapped(xi_first, "xi", XI, 0), swapped(xi_second, "xi", XI, 1),
        around(eta_high, "eta", ETA, 1), around(eta_low, "eta", ETA, -1),
    )
    ft, qe, ce, me = call(
        eta_responses,
        (
            hbm(2, 5, STEPS, 8, LANES), hbm(2, 4, STEPS, 8, LANES),
            vmem(12, 32, LANES), vmem(24, LANES),
        ),
        fe,
        scratch=[pltpu.VMEM((5, LANES, LANES), jnp.float32)],
        name="eta_responses",
    )
    qx, begun = call(xi_responses, (hbm(3, 4, 8, 8, LANES), vmem(XI * 28, LANES)), fx, name="xi_responses")
    part, message = call(
        zeta_local,
        (vmem(5, 64, LANES), vmem(ZETA, 20, 8, LANES)),
        residual, flow, fz, *edges, zeta_gathered, ce, begun,
        scratch=[pltpu.VMEM((5, 64, LANES), jnp.float32)],
        name="zeta_local",
    )
    gathered = exchange(message, "zeta")
    epart, ends_of, message = call(
        eta_local,
        (vmem(3, STEPS, 8, LANES), vmem(4, 32, LANES), vmem(ETA, 40, LANES)),
        part, qz, gathered, zeta_gathered, ft, ce, me,
        scratch=[pltpu.VMEM((3, LANES, LANES), jnp.float32)] * 2,
        name="eta_local",
    )
    gathered = exchange(message, "eta")
    part, message = call(
        xi_local,
        (vmem(5, 8, 8, LANES), vmem(XI * 28, LANES)),
        epart, qe, ce, ends_of, gathered, fx, begun,
        scratch=[
            pltpu.VMEM((4, 32, LANES), jnp.float32),
            pltpu.VMEM((3, LANES, LANES), jnp.float32),
            pltpu.VMEM((3, LANES, LANES), jnp.float32),
        ],
        aliases={6: 1},
        name="xi_local",
    )
    gathered = exchange(message.reshape(XI, 7, 4, LANES), "xi").reshape(XI * 28, LANES)
    incoming = call(
        xi_lines, vmem(XI * 12, LANES), gathered, scratch=[vmem(XI * 8, LANES)], name="xi_lines"
    )
    incoming = exchange(incoming.reshape(XI, 3, 4, LANES), "xi").reshape(XI * 12, LANES)
    update = call(finish, f32(5, 64, LANES), part, qx, incoming, name="finish")
    return update.reshape(5, 8, 8, LANES)


def solution(mesh):
    split = P(None, "zeta", "xi", "eta")
    factor_split = P(None, None, "zeta", "xi", "eta")
    return jax.shard_map(
        on_device,
        mesh=mesh,
        in_specs=(split, split, factor_split, factor_split, factor_split),
        out_specs=split,
        check_vma=False,
    )
```

```python
import jax
import jax.numpy as jnp
from jax import lax
from jax.experimental import pallas as pl
from jax.experimental.pallas import tpu as pltpu
from jax.sharding import PartitionSpec as P

dissipation = 0.05
ZETA, ETA, XI = 4, 8, 16
LANES = 128
field_slot = ((0, 0), (1, 0), (2, 0), (0, 1), (1, 1))
field_group = (0, 0, 0, 1, 2)
CHUNKS = 8
STEPS = LANES // CHUNKS


def f32(*shape):
    return jax.ShapeDtypeStruct(shape, jnp.float32)


def hbm(*shape):
    return pltpu.HBM(shape, jnp.float32)


def vmem(*shape):
    return pltpu.VMEM(shape, jnp.float32)


def call(body, outs, *args, scratch=(), name=None, cost=20000, aliases={}, held=False):
    return pl.pallas_call(
        body,
        out_shape=outs,
        in_specs=[pl.BlockSpec(memory_space=pltpu.HBM if held else pltpu.VMEM)] * len(args),
        out_specs=jax.tree.map(lambda _: pl.BlockSpec(memory_space=pltpu.VMEM), outs),
        scratch_shapes=list(scratch),
        input_output_aliases=aliases,
        name=name,
        cost_estimate=pl.CostEstimate(flops=cost * 1000, bytes_accessed=cost * 100, transcendentals=0),
        compiler_params=pltpu.CompilerParams(vmem_limit_bytes=16 << 20),
    )(*(pltpu.with_memory_space_constraint(arg, pltpu.HBM if held else pltpu.VMEM) for arg in args))


def every(start, stride):
    return pl.ds(start, 8, stride=stride)


def responses(f0, f1, f2, f3, f4):
    n = len(f0)
    forward, back = [], []
    for column in (0, 1):
        ys = []
        for i in range(n):
            if i == 0:
                y = -f0[0] if column == 0 else -f1[0]
            elif i == 1:
                y = -f0[1] * ys[0] - f1[1] if column == 0 else -f0[1] * ys[0]
            else:
                y = -f0[i] * ys[i - 1] - f1[i] * ys[i - 2]
            ys.append(y)
        forward.append(ys)
    for column in (0, 1):
        xs = [None] * n
        for i in reversed(range(n)):
            if i == n - 1:
                x = -f3[i] if column == 0 else -f4[i]
            elif i == n - 2:
                x = -f3[i] * xs[i + 1] - f4[i] if column == 0 else -f3[i] * xs[i + 1]
            else:
                x = -f3[i] * xs[i + 1] - f4[i] * xs[i + 2]
            xs[i] = x
        back.append(xs)
    both = [backward(ys, f2, f3, f4) for ys in forward]
    matrix = [
        forward[0][n - 1], forward[1][n - 1], forward[0][n - 2], forward[1][n - 2],
        back[0][0], back[1][0], back[0][1], back[1][1],
        both[0][0], both[1][0], both[0][1], both[1][1],
    ]
    return back + both, matrix


def backward(ys, f2, f3, f4):
    n = len(ys)
    xs = [None] * n
    for i in reversed(range(n)):
        x = f2[i] * ys[i]
        if i + 1 < n:
            x = x - f3[i] * xs[i + 1]
        if i + 2 < n:
            x = x - f4[i] * xs[i + 2]
        xs[i] = x
    return xs


def solve(vs, f0, f1, f2, f3, f4):
    ys = []
    for i, v in enumerate(vs):
        if i >= 1:
            v = v - f0[i] * ys[i - 1]
        if i >= 2:
            v = v - f1[i] * ys[i - 2]
        ys.append(v)
    xs = backward(ys, f2, f3, f4)
    return xs, (ys[-1], ys[-2], xs[0], xs[1])


def chain(matrices, offsets, first, last):
    n = len(matrices)
    before, after = [], [None] * n
    s1, s2 = first
    for m, o in zip(matrices, offsets):
        before.append((s1, s2))
        n1, n2 = m[0] * s1 + m[1] * s2, m[2] * s1 + m[3] * s2
        s1, s2 = (n1, n2) if o is None else (n1 + o[0], n2 + o[1])
    r1, r2 = last
    for d in reversed(range(n)):
        m, o = matrices[d], offsets[d]
        after[d] = (r1, r2)
        p1, p2 = before[d]
        n1 = m[4] * r1 + m[5] * r2 + (m[8] * p1 + m[9] * p2)
        n2 = m[6] * r1 + m[7] * r2 + (m[10] * p1 + m[11] * p2)
        r1, r2 = (n1, n2) if o is None else (n1 + o[2], n2 + o[3])
    return before, after, (s1, s2), (r1, r2)


def pick(mine, pairs):
    first, second = pairs[0]
    for d in range(1, len(pairs)):
        first = jnp.where(mine == d, pairs[d][0], first)
        second = jnp.where(mine == d, pairs[d][1], second)
    return first, second


def applied(part, response, incoming):
    r1, r2, s1, s2 = incoming
    q1, q2, w1, w2 = response
    return part + (q1 * r1 + q2 * r2) + (w1 * s1 + w2 * s2)


def pack_edges(flow, xi_first, xi_second, eta_low, eta_high):
    xi_odd = lax.rem(lax.axis_index("xi"), 2)
    lane = lax.broadcasted_iota(jnp.int32, (8, LANES), 1)
    low, high = jnp.zeros((8, LANES), jnp.float32), jnp.zeros((8, LANES), jnp.float32)
    for f in range(5):
        for j in range(2):
            before, after = flow[f, every(j, 8), :], flow[f, every(6 + j, 8), :]
            xi_first[2 * f + j] = jnp.where(xi_odd == 1, before, after)
            xi_second[2 * f + j] = jnp.where(xi_odd == 1, after, before)
        for z in range(8):
            k = 8 * f + z
            t = flow[f, pl.ds(8 * z, 8), :]
            here = (lane == 2 * k) | (lane == 2 * k + 1)
            low = jnp.where(here, pltpu.roll(t, (2 * k) % LANES, 1), low)
            high = jnp.where(here, pltpu.roll(t, (2 * k + 2) % LANES, 1), high)
    eta_low[...] = low
    eta_high[...] = high


def zeta_responses(flow_held, fz_held, qz, message, flow, fz, arrived):
    copies = [pltpu.make_async_copy(fz_held.at[g], fz.at[g], arrived.at[g]) for g in range(3)]
    copies.append(pltpu.make_async_copy(flow_held, flow, arrived.at[3]))
    for copy in copies:
        copy.start()
    mine = lax.axis_index("zeta")
    for g in range(3):
        copies[g].wait()
        rows = [[fz[g, c, pl.ds(8 * z, 8), :] for z in range(8)] for c in range(5)]
        response, matrix = responses(*rows)
        for j in range(4):
            for z in range(8):
                qz[g, j, pl.ds(8 * z, 8), :] = response[j][z]
        for k in range(12):
            for d in range(ZETA):
                message[d, 12 * g + k] = matrix[k]
    copies[3].wait()
    for d in range(ZETA):
        place = jnp.where(d > mine, 48, 0)
        for f in range(5):
            for j in range(2):
                message[d, 36 + 2 * f + j] = flow[f, pl.ds(pl.multiple_of(place + 8 * j, 8), 8), :]


def eta_responses(fe, ft, qe, ce, me, turned):
    for p in range(2):
        rows = []
        for c in range(5):
            turned[c] = jnp.concatenate([fe[0, c], fe[1 + p, c]], 0).T
            rows.append([turned[c, every(i, STEPS), :] for i in range(STEPS)])
            for i in range(STEPS):
                ft[p, c, i] = rows[c][i]
        response, matrix = responses(*rows)
        for j in range(4):
            for i in range(STEPS):
                qe[p, j, i] = response[j][i]
        for k in range(12):
            ce[k, every(p, 4), :] = matrix[k]
            ce[k, every(p + 2, 4), :] = matrix[k]
    matrices = [[ce[k, pl.ds(4 * c, 4), :] for k in range(12)] for c in range(CHUNKS)]
    one, zero = jnp.ones((4, LANES), jnp.float32), jnp.zeros((4, LANES), jnp.float32)
    entries = [None] * 12
    for j, unit in enumerate(((one, zero), (zero, one))):
        _, _, (entries[j], entries[2 + j]), (entries[8 + j], entries[10 + j]) = chain(
            matrices, [None] * CHUNKS, unit, (zero, zero)
        )
        _, _, _, (entries[4 + j], entries[6 + j]) = chain(matrices, [None] * CHUNKS, (zero, zero), unit)
    for k in range(12):
        me[pl.ds(2 * k, 2), :] = entries[k][0:2]


def put_halves(message, row, left, right):
    low = lax.broadcasted_iota(jnp.int32, (8, LANES), 1) < 64
    message[every(row, 56), :] = jnp.where(low, left, pltpu.roll(right, 64, 1))
    message[every(28 + row, 56), :] = jnp.where(low, pltpu.roll(left, 64, 1), right)


def xi_responses(fx, qx, message):
    matrices = []
    for g in range(3):
        rows = [[fx[g, c, every(x, 8), :] for x in range(8)] for c in range(5)]
        response, matrix = responses(*rows)
        matrices.append(matrix)
        for j in range(4):
            for x in range(8):
                qx[g, j, x] = response[j][x]
    for k in range(12):
        put_halves(message, k, matrices[0][k], matrices[1][k])
    for k in range(6):
        put_halves(message, 12 + k, matrices[2][k], matrices[2][k + 6])


def zeta_local(residual, flow, fz, xi_second, xi_first, eta_next, eta_prev, zeta_gathered, _, __, part, message, across):
    lane = lax.broadcasted_iota(jnp.int32, (8, LANES), 1)
    zeta, empty = lax.axis_index("zeta"), jnp.zeros((8, LANES), jnp.float32)
    xi_odd, eta = lax.rem(lax.axis_index("xi"), 2) == 1, lax.axis_index("eta")
    before = jnp.where(eta > 0, eta_prev[...], empty)
    after = jnp.where(eta < ETA - 1, eta_next[...], empty)
    low, high = jnp.maximum(zeta - 1, 0), jnp.minimum(zeta + 1, ZETA - 1)
    for f in range(5):
        xs = [jnp.where(xi_odd, xi_first[2 * f + j], xi_second[2 * f + j]) for j in range(2)]
        xs += [flow[f, every(x, 8), :] for x in range(8)]
        xs += [jnp.where(xi_odd, xi_second[2 * f + j], xi_first[2 * f + j]) for j in range(2)]
        for x in range(8):
            across[f, every(x, 8), :] = (
                (xs[x] + xs[x + 4]) - 4.0 * (xs[x + 1] + xs[x + 3]) + 6.0 * xs[x + 2]
            )
        zs = [jnp.where(zeta > 0, zeta_gathered[low, 36 + 2 * f + j], empty) for j in range(2)]
        zs += [flow[f, pl.ds(8 * z, 8), :] for z in range(8)]
        zs += [jnp.where(zeta < ZETA - 1, zeta_gathered[high, 36 + 2 * f + j], empty) for j in range(2)]
        vs = []
        for z in range(8):
            k, t = 8 * f + z, zs[z + 2]
            nxt = pltpu.roll(after, (LANES - 2 * k) % LANES, 1)
            prv = pltpu.roll(before, (LANES - 2 - 2 * k) % LANES, 1)
            up1 = pltpu.roll(jnp.where(lane == 0, nxt, t), LANES - 1, 1)
            up2 = pltpu.roll(jnp.where(lane < 2, nxt, t), LANES - 2, 1)
            down1 = pltpu.roll(jnp.where(lane == LANES - 1, prv, t), 1, 1)
            down2 = pltpu.roll(jnp.where(lane >= LANES - 2, prv, t), 2, 1)
            total = (
                (zs[z] + zs[z + 4] + up2 + down2)
                - 4.0 * (zs[z + 1] + zs[z + 3] + up1 + down1)
                + 12.0 * t
                + across[f, pl.ds(8 * z, 8), :]
            )
            vs.append(residual[f, pl.ds(8 * z, 8), :] - dissipation * total)
        g = field_group[f]
        xs, ends = solve(vs, *[[fz[g, c, pl.ds(8 * z, 8), :] for z in range(8)] for c in range(5)])
        for z in range(8):
            part[f, pl.ds(8 * z, 8), :] = xs[z]
        for v in range(4):
            for d in range(ZETA):
                message[d, 4 * f + v] = ends[v]


def eta_local(part, qz, gathered, matrices, ft, ce, me, epart, ends_of, message, lines, turned):
    mine = lax.axis_index("zeta")
    for f in range(5):
        g = field_group[f]
        before, after, _, _ = chain(
            [[matrices[d, 12 * g + k] for k in range(12)] for d in range(ZETA)],
            [[gathered[d, 4 * f + v] for v in range(4)] for d in range(ZETA)],
            (jnp.zeros((8, LANES), jnp.float32),) * 2,
            (jnp.zeros((8, LANES), jnp.float32),) * 2,
        )
        incoming = pick(mine, after) + pick(mine, before)
        p, half = field_slot[f]
        for z in range(8):
            rows = pl.ds(8 * z, 8)
            lines[p, pl.ds(64 * half + 8 * z, 8), :] = applied(
                part[f, rows, :], [qz[g, j, rows, :] for j in range(4)], incoming
            )
    lines[2, pl.ds(64, 64), :] = jnp.zeros((64, LANES), jnp.float32)
    for p in range(3):
        q = p % 2
        turned[p] = lines[p].T
        vs = [turned[p, every(i, STEPS), :] for i in range(STEPS)]
        xs, ends = solve(vs, *[[ft[q, c, i] for i in range(STEPS)] for c in range(5)])
        for i in range(STEPS):
            epart[p, i] = xs[i]
        for v in range(4):
            ends_of[v, every(p, 4), :] = ends[v]
    zero = jnp.zeros((4, LANES), jnp.float32)
    for v in range(4):
        ends_of[v, every(3, 4), :] = jnp.zeros((8, LANES), jnp.float32)
    _, _, out, back = chain(
        [[ce[k, pl.ds(4 * c, 4), :] for k in range(12)] for c in range(CHUNKS)],
        [[ends_of[v, pl.ds(4 * c, 4), :] for v in range(4)] for c in range(CHUNKS)],
        (zero, zero),
        (zero, zero),
    )
    for d in range(ETA):
        for v, value in enumerate(out + back):
            message[d, pl.ds(4 * v, 4), :] = value
        message[d, pl.ds(16, 24), :] = me[...]


def xi_local(epart, qe, ce, ends_of, gathered, fx, begun, _, part, message, states, turned, lines):
    mine = lax.axis_index("eta")
    zero = jnp.zeros((4, LANES), jnp.float32)
    odd_row = lax.rem(lax.broadcasted_iota(jnp.int32, (4, LANES), 0), 2) == 1

    def entry(d, k):
        even, odd = (jnp.broadcast_to(gathered[d, pl.ds(16 + 2 * k + i, 1), :], (4, LANES)) for i in (0, 1))
        return jnp.where(odd_row, odd, even)

    before, after, _, _ = chain(
        [[entry(d, k) for k in range(12)] for d in range(ETA)],
        [[gathered[d, pl.ds(4 * v, 4), :] for v in range(4)] for d in range(ETA)],
        (zero, zero),
        (zero, zero),
    )
    before, after, _, _ = chain(
        [[ce[k, pl.ds(4 * c, 4), :] for k in range(12)] for c in range(CHUNKS)],
        [[ends_of[v, pl.ds(4 * c, 4), :] for v in range(4)] for c in range(CHUNKS)],
        pick(mine, before),
        pick(mine, after),
    )
    for c in range(CHUNKS):
        for v, value in enumerate(after[c] + before[c]):
            states[v, pl.ds(4 * c, 4), :] = value
    for p in range(3):
        q = p % 2
        incoming = [states[v, every(p, 4), :] for v in range(4)]
        for i in range(STEPS):
            turned[p, every(i, STEPS), :] = applied(epart[p, i], [qe[q, j, i] for j in range(4)], incoming)
        lines[p] = turned[p].T
    all_ends = []
    for f in range(5):
        g = field_group[f]
        p, half = field_slot[f]
        vs = [lines[p, every(64 * half + x, 8), :] for x in range(8)]
        xs, ends = solve(vs, *[[fx[g, c, every(x, 8), :] for x in range(8)] for c in range(5)])
        for x in range(8):
            part[f, x] = xs[x]
        all_ends.append(ends)
    for v in range(4):
        put_halves(message, 18 + v, all_ends[0][v], all_ends[3][v])
        put_halves(message, 22 + v, all_ends[1][v], all_ends[4][v])
    for v in range(2):
        put_halves(message, 26 + v, all_ends[2][v], all_ends[2][v + 2])


def xi_lines(gathered, incoming, turned):
    row = lax.broadcasted_iota(jnp.int32, (3, LANES), 0)
    upper = lax.broadcasted_iota(jnp.int32, (3, LANES), 1) >= 64
    for d in range(XI):
        turned[pl.ds(8 * d, 6), :] = pltpu.roll(gathered[pl.ds(28 * d + 12, 6), :], 64, 1)
        turned[pl.ds(8 * d + 6, 2), :] = pltpu.roll(gathered[pl.ds(28 * d + 26, 2), :], 64, 1)

    def spread(ref, i):
        return jnp.broadcast_to(ref[pl.ds(i, 1), :], (3, LANES))

    def entry(d, k):
        other = spread(turned, 8 * d + k) if k < 6 else spread(gathered, 28 * d + 6 + k)
        return jnp.where((row == 1) & upper, other, spread(gathered, 28 * d + k))

    def offset(d, v):
        if v < 2:
            return gathered[pl.ds(28 * d + 18 + v, 3, stride=4), :]
        last = spread(turned, 8 * d + 4 + v)
        first, second = spread(gathered, 28 * d + 18 + v), spread(gathered, 28 * d + 22 + v)
        return jnp.where(row == 0, first, jnp.where(row == 1, second, last))

    zero = jnp.zeros((3, LANES), jnp.float32)
    before, after, _, _ = chain(
        [[entry(d, k) for k in range(12)] for d in range(XI)],
        [[offset(d, v) for v in range(4)] for d in range(XI)],
        (zero, zero),
        (zero, zero),
    )
    for d in range(XI):
        for v, value in enumerate(after[d] + before[d]):
            incoming[pl.ds(12 * d + v, 3, stride=4), :] = value


def finish(part, qx, incoming, update):
    low = lax.broadcasted_iota(jnp.int32, (8, LANES), 1) < 64
    for f in range(5):
        g = field_group[f]
        p, half = field_slot[f]
        states = []
        for v in range(4):
            near, far = incoming[every(4 * p + v, 24), :], incoming[every(12 + 4 * p + v, 24), :]
            if half == 0:
                states.append(jnp.where(low, near, pltpu.roll(far, 64, 1)))
            else:
                states.append(jnp.where(low, pltpu.roll(near, 64, 1), far))
        for x in range(8):
            update[f, every(x, 8), :] = applied(part[f, x], [qx[g, j, x] for j in range(4)], states)


def swapped(value, axis, count, start):
    pairs = [(i, i + 1) for i in range(start, count - 1, 2)]
    return lax.ppermute(value, axis, pairs + [(j, i) for i, j in pairs])


def around(value, axis, count, step):
    return lax.ppermute(value, axis, [(i, (i + step) % count) for i in range(count)])


def exchange(value, axis):
    return lax.all_to_all(value, axis, 0, 0)


def on_device(residual, flow_state, factors_zeta, factors_eta, factors_xi):
    residual = residual.reshape(5, 64, LANES)
    flow = flow_state.reshape(5, 64, LANES)
    fz, fe, fx = (f.reshape(3, 5, 64, LANES) for f in (factors_zeta, factors_eta, factors_xi))
    qz, message = call(
        zeta_responses,
        (hbm(3, 4, 64, LANES), vmem(ZETA, 46, 8, LANES)),
        flow, fz,
        scratch=[vmem(5, 64, LANES), vmem(3, 5, 64, LANES), pltpu.SemaphoreType.DMA((4,))],
        held=True,
        name="zeta_responses",
    )
    zeta_gathered = exchange(message, "zeta")
    xi_first, xi_second, eta_low, eta_high = call(
        pack_edges, (vmem(10, 8, LANES),) * 2 + (vmem(8, LANES),) * 2, flow, name="pack_edges"
    )
    edges = (
        swapped(xi_second, "xi", XI, 1), swapped(xi_first, "xi", XI, 0),
        around(eta_low, "eta", ETA, -1), around(eta_high, "eta", ETA, 1),
    )
    ft, qe, ce, me = call(
        eta_responses,
        (
            vmem(2, 5, STEPS, 8, LANES), hbm(2, 4, STEPS, 8, LANES),
            vmem(12, 32, LANES), vmem(24, LANES),
        ),
        fe,
        scratch=[pltpu.VMEM((5, LANES, LANES), jnp.float32)],
        name="eta_responses",
    )
    qx, begun = call(xi_responses, (hbm(3, 4, 8, 8, LANES), vmem(XI * 28, LANES)), fx, name="xi_responses")
    part, message = call(
        zeta_local,
        (vmem(5, 64, LANES), vmem(ZETA, 20, 8, LANES)),
        residual, flow, fz, *edges, zeta_gathered, ce, begun,
        scratch=[pltpu.VMEM((5, 64, LANES), jnp.float32)],
        name="zeta_local",
    )
    gathered = exchange(message, "zeta")
    qx_here = pltpu.with_memory_space_constraint(qx, pltpu.VMEM)
    epart, ends_of, message = call(
        eta_local,
        (vmem(3, STEPS, 8, LANES), vmem(4, 32, LANES), vmem(ETA, 40, LANES)),
        part, qz, gathered, zeta_gathered, ft, ce, me,
        scratch=[pltpu.VMEM((3, LANES, LANES), jnp.float32)] * 2,
        name="eta_local",
    )
    gathered = exchange(message, "eta")
    part, message = call(
        xi_local,
        (vmem(5, 8, 8, LANES), vmem(XI * 28, LANES)),
        epart, qe, ce, ends_of, gathered, fx, begun, qx_here,
        scratch=[
            pltpu.VMEM((4, 32, LANES), jnp.float32),
            pltpu.VMEM((3, LANES, LANES), jnp.float32),
            pltpu.VMEM((3, LANES, LANES), jnp.float32),
        ],
        aliases={6: 1},
        name="xi_local",
    )
    gathered = exchange(message.reshape(XI, 7, 4, LANES), "xi").reshape(XI * 28, LANES)
    incoming = call(
        xi_lines, vmem(XI * 12, LANES), gathered, scratch=[vmem(XI * 8, LANES)], name="xi_lines"
    )
    incoming = exchange(incoming.reshape(XI, 3, 4, LANES), "xi").reshape(XI * 12, LANES)
    update = call(finish, f32(5, 64, LANES), part, qx_here, incoming, name="finish")
    return update.reshape(5, 8, 8, LANES)


def solution(mesh):
    split = P(None, "zeta", "xi", "eta")
    factor_split = P(None, None, "zeta", "xi", "eta")
    return jax.shard_map(
        on_device,
        mesh=mesh,
        in_specs=(split, split, factor_split, factor_split, factor_split),
        out_specs=split,
        check_vma=False,
    )
```

```python
import jax
import jax.numpy as jnp
from jax import lax
from jax.experimental import pallas as pl
from jax.experimental.pallas import tpu as pltpu
from jax.sharding import PartitionSpec as P


dissipation = 0.05
ZETA, ETA, XI = 4, 8, 16
LANES = 128
field_slot = ((0, 0), (1, 0), (2, 0), (0, 1), (1, 1))
field_group = (0, 0, 0, 1, 2)
CHUNKS = 8
STEPS = LANES // CHUNKS


def f32(*shape):
    return jax.ShapeDtypeStruct(shape, jnp.float32)


def hbm(*shape):
    return pltpu.HBM(shape, jnp.float32)


def vmem(*shape):
    return pltpu.VMEM(shape, jnp.float32)


def call(body, outs, *args, scratch=(), cost=20000, aliases={}, held=False):
    return pl.pallas_call(
        body,
        out_shape=outs,
        in_specs=[pl.BlockSpec(memory_space=pltpu.HBM if held else pltpu.VMEM)] * len(args),
        out_specs=jax.tree.map(lambda _: pl.BlockSpec(memory_space=pltpu.VMEM), outs),
        scratch_shapes=list(scratch),
        input_output_aliases=aliases,
        cost_estimate=pl.CostEstimate(flops=cost * 1000, bytes_accessed=cost * 100, transcendentals=0),
        compiler_params=pltpu.CompilerParams(vmem_limit_bytes=16 << 20),
    )(*(pltpu.with_memory_space_constraint(arg, pltpu.HBM if held else pltpu.VMEM) for arg in args))


def every(start, stride):
    return pl.ds(start, 8, stride=stride)


def responses(f0, f1, f2, f3, f4):
    n = len(f0)
    forward, back = [], []
    for column in (0, 1):
        ys = []
        for i in range(n):
            if i == 0:
                y = -f0[0] if column == 0 else -f1[0]
            elif i == 1:
                y = -f0[1] * ys[0] - f1[1] if column == 0 else -f0[1] * ys[0]
            else:
                y = -f0[i] * ys[i - 1] - f1[i] * ys[i - 2]
            ys.append(y)
        forward.append(ys)
    for column in (0, 1):
        xs = [None] * n
        for i in reversed(range(n)):
            if i == n - 1:
                x = -f3[i] if column == 0 else -f4[i]
            elif i == n - 2:
                x = -f3[i] * xs[i + 1] - f4[i] if column == 0 else -f3[i] * xs[i + 1]
            else:
                x = -f3[i] * xs[i + 1] - f4[i] * xs[i + 2]
            xs[i] = x
        back.append(xs)
    both = [backward(ys, f2, f3, f4) for ys in forward]
    matrix = [
        forward[0][n - 1], forward[1][n - 1], forward[0][n - 2], forward[1][n - 2],
        back[0][0], back[1][0], back[0][1], back[1][1],
        both[0][0], both[1][0], both[0][1], both[1][1],
    ]
    return back + both, matrix


def backward(ys, f2, f3, f4):
    n = len(ys)
    xs = [None] * n
    for i in reversed(range(n)):
        x = f2[i] * ys[i]
        if i + 1 < n:
            x = x - f3[i] * xs[i + 1]
        if i + 2 < n:
            x = x - f4[i] * xs[i + 2]
        xs[i] = x
    return xs


def solve(vs, f0, f1, f2, f3, f4):
    ys = []
    for i, v in enumerate(vs):
        if i >= 1:
            v = v - f0[i] * ys[i - 1]
        if i >= 2:
            v = v - f1[i] * ys[i - 2]
        ys.append(v)
    xs = backward(ys, f2, f3, f4)
    return xs, (ys[-1], ys[-2], xs[0], xs[1])


def chain(matrices, offsets, first, last):
    n = len(matrices)
    before, after = [], [None] * n
    s1, s2 = first
    for m, o in zip(matrices, offsets):
        before.append((s1, s2))
        n1, n2 = m[0] * s1 + m[1] * s2, m[2] * s1 + m[3] * s2
        s1, s2 = (n1, n2) if o is None else (n1 + o[0], n2 + o[1])
    r1, r2 = last
    for d in reversed(range(n)):
        m, o = matrices[d], offsets[d]
        after[d] = (r1, r2)
        p1, p2 = before[d]
        n1 = m[4] * r1 + m[5] * r2 + (m[8] * p1 + m[9] * p2)
        n2 = m[6] * r1 + m[7] * r2 + (m[10] * p1 + m[11] * p2)
        r1, r2 = (n1, n2) if o is None else (n1 + o[2], n2 + o[3])
    return before, after, (s1, s2), (r1, r2)


def pick(mine, pairs):
    first, second = pairs[0]
    for d in range(1, len(pairs)):
        first = jnp.where(mine == d, pairs[d][0], first)
        second = jnp.where(mine == d, pairs[d][1], second)
    return first, second


def applied(part, response, incoming):
    r1, r2, s1, s2 = incoming
    q1, q2, w1, w2 = response
    return part + (q1 * r1 + q2 * r2) + (w1 * s1 + w2 * s2)


def pack_edges(flow, xi_first, xi_second, eta_low, eta_high):
    xi_odd = lax.rem(lax.axis_index("xi"), 2)
    lane = lax.broadcasted_iota(jnp.int32, (8, LANES), 1)
    low, high = jnp.zeros((8, LANES), jnp.float32), jnp.zeros((8, LANES), jnp.float32)
    for f in range(5):
        for j in range(2):
            before, after = flow[f, every(j, 8), :], flow[f, every(6 + j, 8), :]
            xi_first[2 * f + j] = jnp.where(xi_odd == 1, before, after)
            xi_second[2 * f + j] = jnp.where(xi_odd == 1, after, before)
        for z in range(8):
            k = 8 * f + z
            t = flow[f, pl.ds(8 * z, 8), :]
            here = (lane == 2 * k) | (lane == 2 * k + 1)
            low = jnp.where(here, pltpu.roll(t, (2 * k) % LANES, 1), low)
            high = jnp.where(here, pltpu.roll(t, (2 * k + 2) % LANES, 1), high)
    eta_low[...] = low
    eta_high[...] = high


def zeta_responses(flow_held, fz_held, qz, message, flow, fz, arrived):
    copies = [pltpu.make_async_copy(fz_held.at[g], fz.at[g], arrived.at[g]) for g in range(3)]
    copies.append(pltpu.make_async_copy(flow_held, flow, arrived.at[3]))
    for copy in copies:
        copy.start()
    mine = lax.axis_index("zeta")
    for g in range(3):
        copies[g].wait()
        rows = [[fz[g, c, pl.ds(8 * z, 8), :] for z in range(8)] for c in range(5)]
        response, matrix = responses(*rows)
        for j in range(4):
            for z in range(8):
                qz[g, j, pl.ds(8 * z, 8), :] = response[j][z]
        for k in range(12):
            for d in range(ZETA):
                message[d, 12 * g + k] = matrix[k]
    copies[3].wait()
    for d in range(ZETA):
        place = jnp.where(d > mine, 48, 0)
        for f in range(5):
            for j in range(2):
                message[d, 36 + 2 * f + j] = flow[f, pl.ds(pl.multiple_of(place + 8 * j, 8), 8), :]


def eta_responses(fe, ft, qe, ce, me, turned):
    for p in range(2):
        rows = []
        for c in range(5):
            turned[c] = jnp.concatenate([fe[0, c], fe[1 + p, c]], 0).T
            rows.append([turned[c, every(i, STEPS), :] for i in range(STEPS)])
            for i in range(STEPS):
                ft[p, c, i] = rows[c][i]
        response, matrix = responses(*rows)
        for j in range(4):
            for i in range(STEPS):
                qe[p, j, i] = response[j][i]
        for k in range(12):
            ce[k, every(p, 4), :] = matrix[k]
            ce[k, every(p + 2, 4), :] = matrix[k]
    matrices = [[ce[k, pl.ds(4 * c, 4), :] for k in range(12)] for c in range(CHUNKS)]
    one, zero = jnp.ones((4, LANES), jnp.float32), jnp.zeros((4, LANES), jnp.float32)
    entries = [None] * 12
    for j, unit in enumerate(((one, zero), (zero, one))):
        _, _, (entries[j], entries[2 + j]), (entries[8 + j], entries[10 + j]) = chain(
            matrices, [None] * CHUNKS, unit, (zero, zero)
        )
        _, _, _, (entries[4 + j], entries[6 + j]) = chain(matrices, [None] * CHUNKS, (zero, zero), unit)
    for k in range(12):
        me[pl.ds(2 * k, 2), :] = entries[k][0:2]


def put_halves(message, row, left, right):
    low = lax.broadcasted_iota(jnp.int32, (8, LANES), 1) < 64
    message[every(row, 56), :] = jnp.where(low, left, pltpu.roll(right, 64, 1))
    message[every(28 + row, 56), :] = jnp.where(low, pltpu.roll(left, 64, 1), right)


def xi_responses(fx, qx, message):
    matrices = []
    for g in range(3):
        rows = [[fx[g, c, every(x, 8), :] for x in range(8)] for c in range(5)]
        response, matrix = responses(*rows)
        matrices.append(matrix)
        for j in range(4):
            for x in range(8):
                qx[g, j, x] = response[j][x]
    for k in range(12):
        put_halves(message, k, matrices[0][k], matrices[1][k])
    for k in range(6):
        put_halves(message, 12 + k, matrices[2][k], matrices[2][k + 6])


def zeta_local(residual, flow, fz, eta_next, eta_prev, xi_second, xi_first, zeta_gathered, _, __, part, message, across):
    lane = lax.broadcasted_iota(jnp.int32, (8, LANES), 1)
    zeta, empty = lax.axis_index("zeta"), jnp.zeros((8, LANES), jnp.float32)
    xi_odd, eta = lax.rem(lax.axis_index("xi"), 2) == 1, lax.axis_index("eta")
    before = jnp.where(eta > 0, eta_prev[...], empty)
    after = jnp.where(eta < ETA - 1, eta_next[...], empty)
    low, high = jnp.maximum(zeta - 1, 0), jnp.minimum(zeta + 1, ZETA - 1)
    for f in range(5):
        xs = [jnp.where(xi_odd, xi_first[2 * f + j], xi_second[2 * f + j]) for j in range(2)]
        xs += [flow[f, every(x, 8), :] for x in range(8)]
        xs += [jnp.where(xi_odd, xi_second[2 * f + j], xi_first[2 * f + j]) for j in range(2)]
        for x in range(8):
            across[f, every(x, 8), :] = (
                (xs[x] + xs[x + 4]) - 4.0 * (xs[x + 1] + xs[x + 3]) + 6.0 * xs[x + 2]
            )
        zs = [jnp.where(zeta > 0, zeta_gathered[low, 36 + 2 * f + j], empty) for j in range(2)]
        zs += [flow[f, pl.ds(8 * z, 8), :] for z in range(8)]
        zs += [jnp.where(zeta < ZETA - 1, zeta_gathered[high, 36 + 2 * f + j], empty) for j in range(2)]
        vs = []
        for z in range(8):
            k, t = 8 * f + z, zs[z + 2]
            nxt = pltpu.roll(after, (LANES - 2 * k) % LANES, 1)
            prv = pltpu.roll(before, (LANES - 2 - 2 * k) % LANES, 1)
            up1 = pltpu.roll(jnp.where(lane == 0, nxt, t), LANES - 1, 1)
            up2 = pltpu.roll(jnp.where(lane < 2, nxt, t), LANES - 2, 1)
            down1 = pltpu.roll(jnp.where(lane == LANES - 1, prv, t), 1, 1)
            down2 = pltpu.roll(jnp.where(lane >= LANES - 2, prv, t), 2, 1)
            total = (
                (zs[z] + zs[z + 4] + up2 + down2)
                - 4.0 * (zs[z + 1] + zs[z + 3] + up1 + down1)
                + 12.0 * t
                + across[f, pl.ds(8 * z, 8), :]
            )
            vs.append(residual[f, pl.ds(8 * z, 8), :] - dissipation * total)
        g = field_group[f]
        xs, ends = solve(vs, *[[fz[g, c, pl.ds(8 * z, 8), :] for z in range(8)] for c in range(5)])
        for z in range(8):
            part[f, pl.ds(8 * z, 8), :] = xs[z]
        for v in range(4):
            for d in range(ZETA):
                message[d, 4 * f + v] = ends[v]


def eta_local(part, qz, gathered, matrices, ft, ce, me, epart, ends_of, message, lines, turned):
    mine = lax.axis_index("zeta")
    for f in range(5):
        g = field_group[f]
        before, after, _, _ = chain(
            [[matrices[d, 12 * g + k] for k in range(12)] for d in range(ZETA)],
            [[gathered[d, 4 * f + v] for v in range(4)] for d in range(ZETA)],
            (jnp.zeros((8, LANES), jnp.float32),) * 2,
            (jnp.zeros((8, LANES), jnp.float32),) * 2,
        )
        incoming = pick(mine, after) + pick(mine, before)
        p, half = field_slot[f]
        for z in range(8):
            rows = pl.ds(8 * z, 8)
            lines[p, pl.ds(64 * half + 8 * z, 8), :] = applied(
                part[f, rows, :], [qz[g, j, rows, :] for j in range(4)], incoming
            )
    lines[2, pl.ds(64, 64), :] = jnp.zeros((64, LANES), jnp.float32)
    for p in range(3):
        q = p % 2
        turned[p] = lines[p].T
        vs = [turned[p, every(i, STEPS), :] for i in range(STEPS)]
        xs, ends = solve(vs, *[[ft[q, c, i] for i in range(STEPS)] for c in range(5)])
        for i in range(STEPS):
            epart[p, i] = xs[i]
        for v in range(4):
            ends_of[v, every(p, 4), :] = ends[v]
    zero = jnp.zeros((4, LANES), jnp.float32)
    for v in range(4):
        ends_of[v, every(3, 4), :] = jnp.zeros((8, LANES), jnp.float32)
    _, _, out, back = chain(
        [[ce[k, pl.ds(4 * c, 4), :] for k in range(12)] for c in range(CHUNKS)],
        [[ends_of[v, pl.ds(4 * c, 4), :] for v in range(4)] for c in range(CHUNKS)],
        (zero, zero),
        (zero, zero),
    )
    for d in range(ETA):
        for v, value in enumerate(out + back):
            message[d, pl.ds(4 * v, 4), :] = value
        message[d, pl.ds(16, 24), :] = me[...]


def xi_local(epart, qe, ce, ends_of, gathered, fx, begun, _, part, message, states, turned, lines):
    mine = lax.axis_index("eta")
    zero = jnp.zeros((4, LANES), jnp.float32)
    odd_row = lax.rem(lax.broadcasted_iota(jnp.int32, (4, LANES), 0), 2) == 1

    def entry(d, k):
        even, odd = (jnp.broadcast_to(gathered[d, pl.ds(16 + 2 * k + i, 1), :], (4, LANES)) for i in (0, 1))
        return jnp.where(odd_row, odd, even)

    before, after, _, _ = chain(
        [[entry(d, k) for k in range(12)] for d in range(ETA)],
        [[gathered[d, pl.ds(4 * v, 4), :] for v in range(4)] for d in range(ETA)],
        (zero, zero),
        (zero, zero),
    )
    before, after, _, _ = chain(
        [[ce[k, pl.ds(4 * c, 4), :] for k in range(12)] for c in range(CHUNKS)],
        [[ends_of[v, pl.ds(4 * c, 4), :] for v in range(4)] for c in range(CHUNKS)],
        pick(mine, before),
        pick(mine, after),
    )
    for c in range(CHUNKS):
        for v, value in enumerate(after[c] + before[c]):
            states[v, pl.ds(4 * c, 4), :] = value
    for p in range(3):
        q = p % 2
        incoming = [states[v, every(p, 4), :] for v in range(4)]
        for i in range(STEPS):
            turned[p, every(i, STEPS), :] = applied(epart[p, i], [qe[q, j, i] for j in range(4)], incoming)
        lines[p] = turned[p].T
    all_ends = []
    for f in range(5):
        g = field_group[f]
        p, half = field_slot[f]
        vs = [lines[p, every(64 * half + x, 8), :] for x in range(8)]
        xs, ends = solve(vs, *[[fx[g, c, every(x, 8), :] for x in range(8)] for c in range(5)])
        for x in range(8):
            part[f, x] = xs[x]
        all_ends.append(ends)
    for v in range(4):
        put_halves(message, 18 + v, all_ends[0][v], all_ends[3][v])
        put_halves(message, 22 + v, all_ends[1][v], all_ends[4][v])
    for v in range(2):
        put_halves(message, 26 + v, all_ends[2][v], all_ends[2][v + 2])


def xi_lines(gathered, incoming, turned):
    row = lax.broadcasted_iota(jnp.int32, (3, LANES), 0)
    upper = lax.broadcasted_iota(jnp.int32, (3, LANES), 1) >= 64
    for d in range(XI):
        turned[pl.ds(8 * d, 6), :] = pltpu.roll(gathered[pl.ds(28 * d + 12, 6), :], 64, 1)
        turned[pl.ds(8 * d + 6, 2), :] = pltpu.roll(gathered[pl.ds(28 * d + 26, 2), :], 64, 1)

    def spread(ref, i):
        return jnp.broadcast_to(ref[pl.ds(i, 1), :], (3, LANES))

    def entry(d, k):
        other = spread(turned, 8 * d + k) if k < 6 else spread(gathered, 28 * d + 6 + k)
        return jnp.where((row == 1) & upper, other, spread(gathered, 28 * d + k))

    def offset(d, v):
        if v < 2:
            return gathered[pl.ds(28 * d + 18 + v, 3, stride=4), :]
        last = spread(turned, 8 * d + 4 + v)
        first, second = spread(gathered, 28 * d + 18 + v), spread(gathered, 28 * d + 22 + v)
        return jnp.where(row == 0, first, jnp.where(row == 1, second, last))

    zero = jnp.zeros((3, LANES), jnp.float32)
    before, after, _, _ = chain(
        [[entry(d, k) for k in range(12)] for d in range(XI)],
        [[offset(d, v) for v in range(4)] for d in range(XI)],
        (zero, zero),
        (zero, zero),
    )
    for d in range(XI):
        for v, value in enumerate(after[d] + before[d]):
            incoming[pl.ds(12 * d + v, 3, stride=4), :] = value


def finish(part, qx, incoming, update):
    low = lax.broadcasted_iota(jnp.int32, (8, LANES), 1) < 64
    for f in range(5):
        g = field_group[f]
        p, half = field_slot[f]
        states = []
        for v in range(4):
            near, far = incoming[every(4 * p + v, 24), :], incoming[every(12 + 4 * p + v, 24), :]
            if half == 0:
                states.append(jnp.where(low, near, pltpu.roll(far, 64, 1)))
            else:
                states.append(jnp.where(low, pltpu.roll(near, 64, 1), far))
        for x in range(8):
            update[f, every(x, 8), :] = applied(part[f, x], [qx[g, j, x] for j in range(4)], states)


def swapped(value, axis, count, start):
    pairs = [(i, i + 1) for i in range(start, count - 1, 2)]
    return lax.ppermute(value, axis, pairs + [(j, i) for i, j in pairs])


def around(value, axis, count, step):
    return lax.ppermute(value, axis, [(i, (i + step) % count) for i in range(count)])


def exchange(value, axis):
    return lax.all_to_all(value, axis, 0, 0)


def on_device(residual, flow_state, factors_zeta, factors_eta, factors_xi):
    residual = residual.reshape(5, 64, LANES)
    flow = flow_state.reshape(5, 64, LANES)
    fz, fe, fx = (f.reshape(3, 5, 64, LANES) for f in (factors_zeta, factors_eta, factors_xi))
    qz, message = call(
        zeta_responses,
        (hbm(3, 4, 64, LANES), vmem(ZETA, 46, 8, LANES)),
        flow, fz,
        scratch=[vmem(5, 64, LANES), vmem(3, 5, 64, LANES), pltpu.SemaphoreType.DMA((4,))],
        held=True,
    )
    zeta_gathered = exchange(message, "zeta")
    xi_first, xi_second, eta_low, eta_high = call(
        pack_edges, (vmem(10, 8, LANES),) * 2 + (vmem(8, LANES),) * 2, flow
    )
    eta_next = around(eta_low, "eta", ETA, -1)
    eta_prev = around(eta_high, "eta", ETA, 1)
    xi_two = swapped(xi_second, "xi", XI, 1)
    xi_one = swapped(xi_first, "xi", XI, 0)
    edges = (eta_next, eta_prev, xi_two, xi_one)
    ft, qe, ce, me = call(
        eta_responses,
        (
            vmem(2, 5, STEPS, 8, LANES), hbm(2, 4, STEPS, 8, LANES),
            vmem(12, 32, LANES), vmem(24, LANES),
        ),
        fe,
        scratch=[pltpu.VMEM((5, LANES, LANES), jnp.float32)],
    )
    qx, begun = call(xi_responses, (hbm(3, 4, 8, 8, LANES), vmem(XI * 28, LANES)), fx)
    part, message = call(
        zeta_local,
        (vmem(5, 64, LANES), vmem(ZETA, 20, 8, LANES)),
        residual, flow, fz, *edges, zeta_gathered, ce, begun,
        scratch=[pltpu.VMEM((5, 64, LANES), jnp.float32)],
    )
    gathered = exchange(message, "zeta")
    qx_here = pltpu.with_memory_space_constraint(qx, pltpu.VMEM)
    epart, ends_of, message = call(
        eta_local,
        (vmem(3, STEPS, 8, LANES), vmem(4, 32, LANES), vmem(ETA, 40, LANES)),
        part, qz, gathered, zeta_gathered, ft, ce, me,
        scratch=[pltpu.VMEM((3, LANES, LANES), jnp.float32)] * 2,
    )
    gathered = exchange(message, "eta")
    part, message = call(
        xi_local,
        (vmem(5, 8, 8, LANES), vmem(XI * 28, LANES)),
        epart, qe, ce, ends_of, gathered, fx, begun, qx_here,
        scratch=[
            pltpu.VMEM((4, 32, LANES), jnp.float32),
            pltpu.VMEM((3, LANES, LANES), jnp.float32),
            pltpu.VMEM((3, LANES, LANES), jnp.float32),
        ],
        aliases={6: 1},
    )
    gathered = exchange(message.reshape(XI, 7, 4, LANES), "xi").reshape(XI * 28, LANES)
    incoming = call(xi_lines, vmem(XI * 12, LANES), gathered, scratch=[vmem(XI * 8, LANES)])
    incoming = exchange(incoming.reshape(XI, 3, 4, LANES), "xi").reshape(XI * 12, LANES)
    update = call(finish, f32(5, 64, LANES), part, qx_here, incoming)
    return update.reshape(5, 8, 8, LANES)


def solution(mesh):
    split = P(None, "zeta", "xi", "eta")
    factor_split = P(None, None, "zeta", "xi", "eta")
    return jax.shard_map(
        on_device,
        mesh=mesh,
        in_specs=(split, split, factor_split, factor_split, factor_split),
        out_specs=split,
        check_vma=False,
    )
```
